128 devices in a mesh: seq: 32 (over y, z, core), chan: 4 (over x).
Axes of the slice: x: 4, y: 4, z: 4, core: 2. Of those that a mesh axis runs over, the one named last changes fastest.
Arguments:
- tokens: bfloat16 [4, 8192, 1024], P(None, 'seq', 'chan'), may hold values from -6 to 6
- routing: int32 [8192, 4], P(('seq', 'chan')), may hold values from 0 to 31, as said below
- expert_in: bfloat16 [32, 1024, 4096], P('seq'), may hold values from -0.1875 to 0.1875
- expert_out: bfloat16 [32, 4096, 1024], P('seq'), may hold values from -0.09375 to 0.09375
- gain_mix: float32 [1024], replicated, may hold values from 0.5 to 1.5
- gain_out: float32 [1024], replicated, may hold values from 0.5 to 1.5
Outputs:
- layer_out: bfloat16 [4, 8192, 1024], P(None, ('seq', 'chan'))
The draws below stay inside these ranges and needn't reach their ends.
Inputs may be any that keep to these rules, and one draw needn't show every extreme that they name: Read routing in the order of its flattened index (position, then document). In each aligned block of 256 entries (the tokens of one device along seq+chan) no expert appears more than 24 times, and one expert appears exactly 24 times in every block.
All inputs are finite; a program needn't handle non-finite values.
Results may differ from the reference program's by a relative error of at most 0.0095.
Values may be sent and summed in bfloat16 or wider, within the bound.
No kernel may reach another device: no remote copies, remote signals or barrier semaphores. Data moves between devices by JAX's collectives and lax.ppermute only.
A program may use at most 128 MiB of HBM per device.

```python
import math
import jax
import jax.numpy as jnp
from jax import lax

D = 1024
FF = 4096
L = 8192
DOCS = 4
EXPERT_TOTAL = 32
ROWS_DEV = 256
EXPERT_CAPACITY = 24


def draw_routing(key, part):
    blocks = L * DOCS // ROWS_DEV
    random_key_favored, random_key_credit, random_key_blocks = jax.random.split(key, 3)
    hot_expert = jax.random.randint(random_key_favored, (), 0, EXPERT_TOTAL).astype(jnp.int32)
    extra_credit_list = jax.random.randint(random_key_credit, (EXPERT_TOTAL,), 0, 4).astype(jnp.int32) * 65536
    position_expert = jnp.repeat(jnp.arange(EXPERT_TOTAL, dtype=jnp.int32), EXPERT_CAPACITY)

    def one_block(index):
        block_key = jax.random.fold_in(random_key_blocks, index)
        random_key_rating, key_order = jax.random.split(block_key)
        router_scores = jax.random.randint(random_key_rating, (EXPERT_TOTAL * EXPERT_CAPACITY,), 0, 262144).astype(jnp.int32) + extra_credit_list[position_expert]
        router_scores = jnp.where(position_expert == hot_expert, -1, router_scores)
        ranking = jnp.argsort(-router_scores, stable=True)
        chosen = position_expert[ranking[:ROWS_DEV - EXPERT_CAPACITY]]
        labels = jnp.concatenate([jnp.full((EXPERT_CAPACITY,), hot_expert, jnp.int32), chosen])
        return jax.random.permutation(key_order, labels)
    grid = jax.vmap(one_block)(jnp.arange(blocks, dtype=jnp.int32))
    return grid.reshape(L, DOCS).astype(jnp.int32)


def block_levels(rng, extent, cuts, least, top_value):
    def one(dim, shards_of):
        steps = jax.random.uniform(jax.random.fold_in(jax.random.fold_in(rng, 6), dim), (shards_of,), jnp.float32, least / len(cuts), top_value / len(cuts))
        return jnp.repeat(jnp.exp(steps), extent[dim] // shards_of).reshape((-1,) + (1,) * (len(extent) - dim - 1))

    gain = one(*cuts[0])
    for cut in cuts[1:]:
        gain = gain * one(*cut)
    return gain


def normal_values(key, extent, width, reach, cuts=(), kind=jnp.bfloat16):
    gain = block_levels(key, extent, cuts, -0.22, 0.18) if cuts else 1.0
    array = jax.random.normal(key, extent, jnp.float32) * width * gain
    return jnp.minimum(jnp.maximum(array, -reach), reach).astype(kind)


def setup_inputs(seed: int = 0) -> dict:
    key_list = jax.random.split(jax.random.key(seed), 7)
    tokens = normal_values(key_list[0], (DOCS, L, D), 1.0, 6.0, ((1, 32), (2, 4)))
    routing = draw_routing(jax.random.fold_in(key_list[6], 71), 0)
    expert_in = normal_values(key_list[2], (EXPERT_TOTAL, D, FF), D ** -0.5, 0.1875, ((0, 32),))
    expert_out = normal_values(key_list[3], (EXPERT_TOTAL, FF, D), FF ** -0.5, 0.09375, ((0, 32),))
    gain_mix = jnp.clip(1.0 + 0.1 * jax.random.normal(key_list[4], (D,), jnp.float32), 0.5, 1.5)
    gain_out = jnp.clip(1.0 + 0.1 * jax.random.normal(key_list[5], (D,), jnp.float32), 0.5, 1.5)
    return {"tokens": tokens, "routing": routing, "expert_in": expert_in, "expert_out": expert_out, "gain_mix": gain_mix, "gain_out": gain_out}


def hidden_table(freq_list, full_width):
    inputs = jnp.arange(full_width, dtype=jnp.int32)
    product = freq_list[:, None] * inputs[None, :] % full_width
    angles = product.astype(jnp.float32) * (2.0 * math.pi / full_width)
    factor = 1.0 / math.sqrt(full_width)
    return jnp.concatenate([jnp.cos(angles) * factor, -jnp.sin(angles) * factor], axis=0).astype(jnp.bfloat16)

def layer_norm(values, gain_vec):
    center = values - lax.optimization_barrier(jnp.mean(values, axis=-1, keepdims=True))
    spread = lax.optimization_barrier(jnp.mean(center * center, axis=-1, keepdims=True))
    return center * lax.rsqrt(spread + 1e-05) * gain_vec

def settle(values):
    return lax.optimization_barrier(values)

def reference(tokens, routing, expert_in, expert_out, gain_mix, gain_out):
    doc_count, seq_len, full_width = tokens.shape
    rows_all = tokens.reshape(doc_count * seq_len, full_width)
    dft_table = hidden_table(jnp.arange(full_width, dtype=jnp.int32), full_width)
    spectrum = lax.dot_general(rows_all, dft_table, (((1,), (1,)), ((), ())), preferred_element_type=jnp.float32).astype(jnp.bfloat16)
    spectrum = settle(spectrum).astype(jnp.float32)
    real_part = spectrum[:, :full_width].reshape(doc_count, seq_len, full_width)
    imag_part = spectrum[:, full_width:].reshape(doc_count, seq_len, full_width)
    transformed = jnp.fft.fft(lax.complex(real_part, imag_part), axis=1)
    mixing = (jnp.real(transformed) * (1.0 / math.sqrt(seq_len))).astype(jnp.bfloat16)
    summed = tokens.astype(jnp.float32) + settle(mixing).astype(jnp.float32)
    normed = layer_norm(summed, gain_mix).astype(jnp.bfloat16).reshape(doc_count * seq_len, full_width)
    expert_ids = routing.T.reshape(doc_count * seq_len)
    slots = doc_count * seq_len // ROWS_DEV * EXPERT_CAPACITY

    def one_expert(totals, expert):
        chosen = expert_ids == expert
        picked = jnp.nonzero(chosen, size=slots, fill_value=0)[0]
        filled = (jnp.arange(slots) < jnp.sum(chosen.astype(jnp.int32))).astype(jnp.float32)
        hidden = jax.nn.gelu(jnp.dot(normed[picked], expert_in[expert], preferred_element_type=jnp.float32)).astype(jnp.bfloat16)
        result = jnp.dot(hidden, expert_out[expert], preferred_element_type=jnp.float32).astype(jnp.bfloat16)
        result = settle(result).astype(jnp.float32) * filled[:, None]
        return (totals.at[picked].add(result), None)
    totals = jnp.zeros((doc_count * seq_len, full_width), jnp.float32)
    totals, unused = lax.scan(one_expert, totals, jnp.arange(EXPERT_TOTAL, dtype=jnp.int32))
    result = layer_norm(settle(normed).astype(jnp.float32) + totals, gain_out)
    return result.astype(jnp.bfloat16).reshape(doc_count, seq_len, full_width)
```

```python
import math

import jax
import jax.numpy as jnp
import numpy as np
from jax import lax
from jax.experimental import pallas as pl
from jax.experimental.pallas import tpu as pltpu
from jax.sharding import Mesh
from jax.sharding import PartitionSpec as P

SEQ = ("seq_0", "seq_1", "seq_2")
SEQ_CHAN = ("seq_0", "seq_1", "seq_2", "chan")

D = 1024
L = 8192
DOCS = 4
N_SEQ = 32
N_CHAN = 4
N_ALL = N_SEQ * N_CHAN
POS = L // N_SEQ
CH = D // N_CHAN
QUARTER = POS // N_CHAN
ROWS = DOCS * QUARTER
CH_OWN = CH // N_SEQ
SLOTS = 24
F32 = jnp.float32
BF16 = jnp.bfloat16
NN = (((1,), (0,)), ((), ()))
NT = (((1,), (1,)), ((), ()))
TN = (((0,), (0,)), ((), ()))


def mm(a, b, dims):
    return lax.dot_general(a, b, dims, preferred_element_type=F32)


def kernel_params(mib=48):
    return pltpu.CompilerParams(vmem_limit_bytes=mib << 20)


def twiddle_tables():
    k = np.arange(N_SEQ)[:, None]
    j = np.arange(POS)[None, :]
    angle = 2.0 * np.pi * ((k * j) % L) / L
    scale = 1.0 / math.sqrt(L)
    return (
        (np.cos(angle) * scale).astype(np.float32),
        (-np.sin(angle) * scale).astype(np.float32),
    )


def position_table():
    j = np.arange(POS)
    m = (np.arange(2)[:, None] + 2 * np.arange(POS // 2)[None, :]).reshape(-1)
    angle = 2.0 * np.pi * ((m[:, None] * j[None, :]) % POS) / POS
    cos, sin = np.cos(angle), np.sin(angle)
    return np.concatenate(
        [np.concatenate([cos, sin], 1), np.concatenate([sin, -cos], 1)], 0
    ).astype(BF16)


def hidden_tables():
    ch = np.arange(CH_OWN)[:, None, None]
    seq = np.arange(N_SEQ)[None, :, None]
    chan = np.arange(N_CHAN)[None, None, :]
    d = (chan * CH + seq * CH_OWN + ch).reshape(-1)
    f = np.arange(D // 2)
    angle = 2.0 * np.pi * ((d[:, None] * f[None, :]) % D) / D
    scale = 1.0 / math.sqrt(D)
    return (np.cos(angle) * scale).astype(BF16), (-np.sin(angle) * scale).astype(BF16)


def split_kernel(tok_ref, col_ref, row_ref):
    eye = (
        lax.broadcasted_iota(jnp.int32, (CH, CH), 0)
        == lax.broadcasted_iota(jnp.int32, (CH, CH), 1)
    ).astype(BF16)
    for pair in range(DOCS // 2):
        flipped = [
            mm(eye, tok_ref[2 * pair + i], NT).reshape(N_SEQ, CH_OWN, POS) for i in range(2)
        ]
        both = jnp.concatenate(flipped, axis=1).astype(BF16)
        col_ref[:, 2 * CH_OWN * pair : 2 * CH_OWN * (pair + 1), :] = both
    for q in range(N_CHAN):
        for doc in range(DOCS):
            row_ref[q, doc * QUARTER : (doc + 1) * QUARTER, :] = tok_ref[
                doc, q * QUARTER : (q + 1) * QUARTER, :
            ]


def split_tokens(tokens):
    return pl.pallas_call(
        split_kernel,
        out_shape=(
            jax.ShapeDtypeStruct((N_SEQ, DOCS * CH_OWN, POS), BF16),
            jax.ShapeDtypeStruct((N_CHAN, ROWS, CH), BF16),
        ),
        compiler_params=kernel_params(),
        name="split_tokens",
    )(tokens)


def real_fft(x):
    n = len(x)
    if n == 1:
        return [(x[0], None)]
    even = real_fft(x[0::2])
    odd = real_fft(x[1::2])
    if n == 2:
        return [(even[0][0] + odd[0][0], None), (even[0][0] - odd[0][0], None)]
    out = [None] * (n // 2 + 1)
    for k in range(n // 4 + 1):
        er, ei = even[k]
        orr, oi = odd[k]
        if k == 0:
            out[0] = (er + orr, None)
            out[n // 2] = (er - orr, None)
        elif 4 * k == n:
            out[k] = (er, -orr)
        else:
            c = math.cos(2.0 * math.pi * k / n)
            s = -math.sin(2.0 * math.pi * k / n)
            if 8 * k == n:
                tr, ti = (orr + oi) * c, (oi - orr) * c
            else:
                tr, ti = orr * c - oi * s, orr * s + oi * c
            out[k] = (er + tr, ei + ti)
            out[n // 2 - k] = (er - tr, ti - ei)
    return out


def sequence_kernel(x_ref, twr_ref, twi_ref, tab_ref, out_ref, t_ref, s_ref):
    for doc in range(DOCS):
        for half in range(POS // 128):
            lanes = slice(half * 128, (half + 1) * 128)
            lanes_im = slice(POS + half * 128, POS + (half + 1) * 128)
            rows = slice(doc * CH_OWN, (doc + 1) * CH_OWN)
            freq = real_fft([x_ref[s, rows, lanes].astype(F32) for s in range(N_SEQ)])
            for k in range(N_SEQ):
                if k <= N_SEQ // 2:
                    fr, fi = freq[k]
                else:
                    fr, fi = freq[N_SEQ - k]
                    fi = -fi
                wr = twr_ref[k : k + 1, lanes]
                wi = twi_ref[k : k + 1, lanes]
                if fi is None:
                    tr, ti = fr * wr, fr * wi
                else:
                    tr, ti = fr * wr - fi * wi, fr * wi + fi * wr
                t_ref[doc, k * CH_OWN : (k + 1) * CH_OWN, lanes] = tr
                t_ref[doc, k * CH_OWN : (k + 1) * CH_OWN, lanes_im] = ti
    for doc in range(DOCS):
        part = mm(tab_ref[...], t_ref[doc].astype(BF16), NT)
        for i in range(4):
            for h in range(2):
                s_ref[h, pl.ds(4 * i + doc, N_ALL, stride=16), :] = part[
                    i * N_ALL : (i + 1) * N_ALL, h * 128 : (h + 1) * 128
                ]
    for h in range(2):
        out_ref[:, :, h * 128 : (h + 1) * 128] = s_ref[h].reshape(N_ALL, 16, 128).astype(BF16)


def sequence_sums(cols):
    twr, twi = twiddle_tables()
    return pl.pallas_call(
        sequence_kernel,
        out_shape=jax.ShapeDtypeStruct((N_ALL, 16, N_SEQ * CH_OWN), BF16),
        scratch_shapes=[
            pltpu.VMEM((DOCS, N_SEQ * CH_OWN, 2 * POS), F32),
            pltpu.VMEM((2, N_ALL * 16, 128), F32),
        ],
        compiler_params=kernel_params(),
        name="sequence_sums",
    )(cols, jnp.asarray(twr), jnp.asarray(twi), jnp.asarray(position_table()))


def norm_rows(values, gain):
    center = values - jnp.mean(values, axis=-1, keepdims=True)
    spread = jnp.mean(center * center, axis=-1, keepdims=True)
    return center * lax.rsqrt(spread + 1e-05) * gain


def slot_map(ids):
    one = (lax.broadcasted_iota(jnp.int32, (N_SEQ, ROWS), 0) == ids).astype(F32)
    earlier = (
        lax.broadcasted_iota(jnp.int32, (ROWS, ROWS), 0)
        < lax.broadcasted_iota(jnp.int32, (ROWS, ROWS), 1)
    ).astype(BF16)
    before = mm(one.astype(BF16), earlier, NN)
    rank = jnp.sum(before * one, axis=0, keepdims=True).astype(jnp.int32)
    target = ids * SLOTS + rank
    slots = lax.broadcasted_iota(jnp.int32, (N_SEQ * SLOTS, ROWS), 0)
    return (slots == target).astype(BF16)


def mix_kernel(r_ref, res_ref, ids_ref, tc_ref, ts_ref, gain_ref, normed_ref, out_ref, s_ref, a_ref):
    lanes = N_SEQ * CH_OWN
    for h in range(2):
        s_ref[h] = r_ref[:, :, h * 128 : (h + 1) * 128].astype(F32).reshape(N_ALL * 16, 128)
    row = lax.broadcasted_iota(jnp.int32, (lanes, lanes), 0)
    col = lax.broadcasted_iota(jnp.int32, (lanes, lanes), 1)
    perm = ((row % N_SEQ == col // CH_OWN) & (row // N_SEQ == col % CH_OWN)).astype(BF16)
    for r in range(16):
        part, parity, doc = r // 8, (r // 4) % 2, r % 4
        block = jnp.concatenate(
            [s_ref[h, pl.ds(r, N_ALL, stride=16), :] for h in range(2)], axis=1
        ).astype(BF16)
        flipped = mm(perm, block, NT).astype(BF16)
        at = (doc * 2 + parity) * N_SEQ
        for ch in range(CH_OWN):
            base = part * D + ch * N_ALL
            a_ref[at : at + N_SEQ, base : base + N_ALL] = flipped[ch * N_SEQ : (ch + 1) * N_SEQ]
    cos_part = mm(a_ref[:, :D], tc_ref[...], NN)
    sin_part = mm(a_ref[:, D:], ts_ref[...], NN)
    half = D // 2
    sign = jnp.where(
        (lax.broadcasted_iota(jnp.int32, (D, 128), 0) // N_ALL) % 2 == 0, 1.0, -1.0
    ) * (1.0 / math.sqrt(D))
    middle = mm(a_ref[:, :D], sign.astype(BF16), NN)[:, :1]
    mirror = (
        lax.broadcasted_iota(jnp.int32, (half, half), 0)
        + lax.broadcasted_iota(jnp.int32, (half, half), 1)
        == half
    ).astype(BF16)
    low = (cos_part + sin_part).astype(BF16).astype(F32)
    high = mm((cos_part - sin_part).astype(BF16), mirror, NN)
    first = lax.broadcasted_iota(jnp.int32, (ROWS, half), 1) == 0
    high = jnp.where(first, middle.astype(BF16).astype(F32), high)
    mixing = jnp.concatenate([low, high], axis=1)
    residual = jnp.concatenate([res_ref[c].astype(F32) for c in range(N_CHAN)], axis=1)
    normed = norm_rows(residual + mixing, gain_ref[...]).astype(BF16)
    normed_ref[...] = normed
    out_ref[...] = mm(slot_map(ids_ref[...]), normed, NN).astype(BF16)


def mix_rows(parts, residual, ids, gain):
    tc, ts = hidden_tables()
    return pl.pallas_call(
        mix_kernel,
        out_shape=(
            jax.ShapeDtypeStruct((ROWS, D), BF16),
            jax.ShapeDtypeStruct((N_SEQ * SLOTS, D), BF16),
        ),
        scratch_shapes=[
            pltpu.VMEM((2, N_ALL * 16, 128), F32),
            pltpu.VMEM((ROWS, 2 * D), BF16),
        ],
        compiler_params=kernel_params(),
        name="mix_rows",
    )(parts, residual, ids, jnp.asarray(tc), jnp.asarray(ts), gain)


def finish_kernel(back_ref, normed_ref, ids_ref, gain_ref, out_ref):
    combined = mm(slot_map(ids_ref[...]), back_ref[...], TN)
    values = norm_rows(normed_ref[...].astype(F32) + combined, gain_ref[...])
    out_ref[...] = values.astype(BF16)


def finish_rows(back, normed, ids, gain):
    return pl.pallas_call(
        finish_kernel,
        out_shape=jax.ShapeDtypeStruct((ROWS, D), BF16),
        compiler_params=kernel_params(),
        name="finish_rows",
    )(back, normed, ids, gain)


def exchange(x, axes):
    return lax.all_to_all(x, axes, split_axis=0, concat_axis=0, tiled=True)


def local(tokens, routing, expert_in, expert_out, gain_mix, gain_out):
    ids = routing.T.reshape(1, ROWS)
    cols, rows = split_tokens(tokens)
    columns = exchange(cols, SEQ)
    residual = exchange(rows, "chan")
    parts = exchange(sequence_sums(columns), SEQ_CHAN)
    normed, outgoing = mix_rows(parts, residual, ids, gain_mix.reshape(1, D))
    slots = exchange(outgoing.reshape(N_SEQ, SLOTS, D), SEQ)
    inputs = slots.reshape(N_SEQ * SLOTS, D)
    hidden = jax.nn.gelu(mm(inputs, expert_in[0], NN)).astype(BF16)
    result = mm(hidden, expert_out[0], NN).astype(BF16)
    back = exchange(result.reshape(N_SEQ, SLOTS, D), SEQ)
    out = finish_rows(back.reshape(N_SEQ * SLOTS, D), normed, ids, gain_out.reshape(1, D))
    return out.reshape(DOCS, QUARTER, D)


def solution(mesh):
    torus = Mesh(
        mesh.devices.reshape(4, 4, 2, mesh.shape["chan"]), ("seq_0", "seq_1", "seq_2", "chan")
    )
    return jax.shard_map(
        local,
        mesh=torus,
        in_specs=(
            P(None, SEQ, "chan"),
            P(SEQ_CHAN, None),
            P(SEQ, None, None),
            P(SEQ, None, None),
            P(),
            P(),
        ),
        out_specs=P(None, SEQ_CHAN, None),
        check_vma=False,
    )
```

```python
import math

import jax
import jax.numpy as jnp
import numpy as np
from jax import lax
from jax.experimental import pallas as pl
from jax.experimental.pallas import tpu as pltpu
from jax.sharding import Mesh
from jax.sharding import PartitionSpec as P

SEQ = ("seq_0", "seq_1", "seq_2")
SEQ_CHAN = ("seq_0", "seq_1", "seq_2", "chan")

D = 1024
L = 8192
DOCS = 4
N_SEQ = 32
N_CHAN = 4
N_ALL = N_SEQ * N_CHAN
POS = L // N_SEQ
CH = D // N_CHAN
QUARTER = POS // N_CHAN
ROWS = DOCS * QUARTER
CH_OWN = CH // N_SEQ
CHUNKS = ((0, 24),)
F32 = jnp.float32
BF16 = jnp.bfloat16
NN = (((1,), (0,)), ((), ()))
NT = (((1,), (1,)), ((), ()))
TN = (((0,), (0,)), ((), ()))


def mm(a, b, dims):
    return lax.dot_general(a, b, dims, preferred_element_type=F32)


def in_hbm(x):
    return pltpu.with_memory_space_constraint(x, pltpu.HBM)


def kernel_params(mib):
    return pltpu.CompilerParams(vmem_limit_bytes=mib << 20)


def twiddle_tables():
    k = np.arange(N_SEQ)[:, None]
    j = np.arange(POS)[None, :]
    angle = 2.0 * np.pi * ((k * j) % L) / L
    scale = 1.0 / math.sqrt(L)
    return (
        (np.cos(angle) * scale).astype(np.float32),
        (-np.sin(angle) * scale).astype(np.float32),
    )


def position_table():
    j = np.arange(POS)
    m = (np.arange(2)[:, None] + 2 * np.arange(POS // 2)[None, :]).reshape(-1)
    angle = 2.0 * np.pi * ((m[:, None] * j[None, :]) % POS) / POS
    cos, sin = np.cos(angle), np.sin(angle)
    return np.concatenate(
        [np.concatenate([cos, sin], 1), np.concatenate([sin, -cos], 1)], 0
    ).astype(BF16)


def tables_kernel(tc_ref, ts_ref):
    block = 128
    f = lax.broadcasted_iota(jnp.int32, (block, D // 2), 1)
    for i in range(D // block):
        row = lax.broadcasted_iota(jnp.int32, (block, D // 2), 0) + i * block
        ch, owner = row // N_ALL, row % N_ALL
        d = owner % N_CHAN * CH + owner // N_CHAN * CH_OWN + ch
        turn = (d * f) % D
        turn = jnp.where(turn >= D // 2, turn - D, turn)
        angle = turn.astype(F32) * (2.0 * math.pi / D)
        factor = 1.0 / math.sqrt(D)
        rows = slice(i * block, (i + 1) * block)
        tc_ref[rows, :] = (jnp.cos(angle) * factor).astype(BF16)
        ts_ref[rows, :] = (-jnp.sin(angle) * factor).astype(BF16)


def hidden_tables():
    return pl.pallas_call(
        tables_kernel,
        out_shape=(jax.ShapeDtypeStruct((D, D // 2), BF16),) * 2,
        compiler_params=kernel_params(8),
        name="hidden_tables",
    )()


def split_kernel(chan_ref, tok_ref, *refs):
    n = (len(refs) - 2 - N_CHAN) // 2
    tables, col_ref, row_refs = refs[:n], refs[n], refs[n + 1 : n + 1 + N_CHAN]
    copies, sem = refs[n + 1 + N_CHAN : -1], refs[-1]
    moves = [
        pltpu.make_async_copy(src, dst, sem.at[i])
        for i, (src, dst) in enumerate(zip(tables, copies))
    ]
    for move in moves:
        move.start()
    eye = (
        lax.broadcasted_iota(jnp.int32, (CH, CH), 0)
        == lax.broadcasted_iota(jnp.int32, (CH, CH), 1)
    ).astype(BF16)
    for pair in range(DOCS // 2):
        flipped = [
            mm(eye, tok_ref[2 * pair + i], NT).reshape(N_SEQ, CH_OWN, POS) for i in range(2)
        ]
        both = jnp.concatenate(flipped, axis=1).astype(BF16)
        col_ref[:, 2 * CH_OWN * pair : 2 * CH_OWN * (pair + 1), :] = both
    for i, row_ref in enumerate(row_refs):
        first = pl.multiple_of((chan_ref[0] + i) % N_CHAN * QUARTER, QUARTER)
        for doc in range(DOCS):
            row_ref[doc * QUARTER : (doc + 1) * QUARTER, :] = tok_ref[
                doc, pl.ds(first, QUARTER), :
            ]
    for move in moves:
        move.wait()


def split_tokens(chan_pos, tokens, *tables):
    cols, *rest = pl.pallas_call(
        split_kernel,
        out_shape=(
            jax.ShapeDtypeStruct((N_SEQ, DOCS * CH_OWN, POS), BF16),
            *(jax.ShapeDtypeStruct((ROWS, CH), BF16) for _ in range(N_CHAN)),
            *(jax.ShapeDtypeStruct(t.shape, t.dtype) for t in tables),
        ),
        in_specs=[pl.BlockSpec(memory_space=pltpu.SMEM), pl.BlockSpec(memory_space=pltpu.VMEM)]
        + [pl.BlockSpec(memory_space=pltpu.HBM)] * len(tables),
        scratch_shapes=[pltpu.SemaphoreType.DMA((len(tables),))],
        compiler_params=kernel_params(8),
        name="split_tokens",
    )(chan_pos, tokens, *map(in_hbm, tables))
    return cols, rest[:N_CHAN], rest[N_CHAN:]


def real_fft(x):
    n = len(x)
    if n == 1:
        return [(x[0], None)]
    even = real_fft(x[0::2])
    odd = real_fft(x[1::2])
    if n == 2:
        return [(even[0][0] + odd[0][0], None), (even[0][0] - odd[0][0], None)]
    out = [None] * (n // 2 + 1)
    for k in range(n // 4 + 1):
        er, ei = even[k]
        orr, oi = odd[k]
        if k == 0:
            out[0] = (er + orr, None)
            out[n // 2] = (er - orr, None)
        elif 4 * k == n:
            out[k] = (er, -orr)
        else:
            c = math.cos(2.0 * math.pi * k / n)
            s = -math.sin(2.0 * math.pi * k / n)
            if 8 * k == n:
                tr, ti = (orr + oi) * c, (oi - orr) * c
            else:
                tr, ti = orr * c - oi * s, orr * s + oi * c
            out[k] = (er + tr, ei + ti)
            out[n // 2 - k] = (er - tr, ti - ei)
    return out


def sequence_kernel(x_ref, twr_ref, twi_ref, tab_ref, out_ref, t_ref, s_ref):
    for doc in range(DOCS):
        for half in range(POS // 128):
            lanes = slice(half * 128, (half + 1) * 128)
            lanes_im = slice(POS + half * 128, POS + (half + 1) * 128)
            rows = slice(doc * CH_OWN, (doc + 1) * CH_OWN)
            freq = real_fft([x_ref[s, rows, lanes].astype(F32) for s in range(N_SEQ)])
            for k in range(N_SEQ):
                if k <= N_SEQ // 2:
                    fr, fi = freq[k]
                else:
                    fr, fi = freq[N_SEQ - k]
                    fi = -fi
                wr = twr_ref[k : k + 1, lanes]
                wi = twi_ref[k : k + 1, lanes]
                if fi is None:
                    tr, ti = fr * wr, fr * wi
                else:
                    tr, ti = fr * wr - fi * wi, fr * wi + fi * wr
                t_ref[doc, k * CH_OWN : (k + 1) * CH_OWN, lanes] = tr
                t_ref[doc, k * CH_OWN : (k + 1) * CH_OWN, lanes_im] = ti
    for doc in range(DOCS):
        part = mm(tab_ref[...], t_ref[doc].astype(BF16), NT)
        for i in range(4):
            for h in range(2):
                s_ref[h, pl.ds(4 * i + doc, N_ALL, stride=16), :] = part[
                    i * N_ALL : (i + 1) * N_ALL, h * 128 : (h + 1) * 128
                ]
    for h in range(2):
        out_ref[:, :, h * 128 : (h + 1) * 128] = s_ref[h].reshape(N_ALL, 16, 128).astype(BF16)


def sequence_sums(cols, twr, twi, tab):
    return pl.pallas_call(
        sequence_kernel,
        out_shape=jax.ShapeDtypeStruct((N_ALL, 16, N_SEQ * CH_OWN), BF16),
        scratch_shapes=[
            pltpu.VMEM((DOCS, N_SEQ * CH_OWN, 2 * POS), F32),
            pltpu.VMEM((2, N_ALL * 16, 128), F32),
        ],
        compiler_params=kernel_params(24),
        name="sequence_sums",
    )(cols, twr, twi, tab)


def norm_rows(values, gain):
    center = values - jnp.mean(values, axis=-1, keepdims=True)
    spread = jnp.mean(center * center, axis=-1, keepdims=True)
    return center * lax.rsqrt(spread + 1e-05) * gain


def slot_maps(ids):
    one = (lax.broadcasted_iota(jnp.int32, (N_SEQ, ROWS), 0) == ids).astype(F32)
    earlier = (
        lax.broadcasted_iota(jnp.int32, (ROWS, ROWS), 0)
        < lax.broadcasted_iota(jnp.int32, (ROWS, ROWS), 1)
    ).astype(BF16)
    before = mm(one.astype(BF16), earlier, NN)
    rank = jnp.sum(before * one, axis=0, keepdims=True).astype(jnp.int32)
    maps = []
    for start, count in CHUNKS:
        inside = (rank >= start) & (rank < start + count)
        target = jnp.where(inside, ids * count + rank - start, -1)
        slots = lax.broadcasted_iota(jnp.int32, (N_SEQ * count, ROWS), 0)
        maps.append((slots == target).astype(BF16))
    return maps


def mix_kernel(chan_ref, r_ref, *refs):
    res_refs, (ids_ref, tc_ref, ts_ref, gain_ref, normed_ref) = refs[:N_CHAN], refs[N_CHAN : N_CHAN + 5]
    *out_refs, s_ref, a_ref, x_ref = refs[N_CHAN + 5 :]
    for i, res_ref in enumerate(res_refs):
        x_ref[(chan_ref[0] + N_CHAN - i) % N_CHAN] = res_ref[...]
    lanes = N_SEQ * CH_OWN
    for h in range(2):
        s_ref[h] = r_ref[:, :, h * 128 : (h + 1) * 128].astype(F32).reshape(N_ALL * 16, 128)
    row = lax.broadcasted_iota(jnp.int32, (lanes, lanes), 0)
    col = lax.broadcasted_iota(jnp.int32, (lanes, lanes), 1)
    perm = ((row % N_SEQ == col // CH_OWN) & (row // N_SEQ == col % CH_OWN)).astype(BF16)
    for r in range(16):
        part, parity, doc = r // 8, (r // 4) % 2, r % 4
        block = jnp.concatenate(
            [s_ref[h, pl.ds(r, N_ALL, stride=16), :] for h in range(2)], axis=1
        ).astype(BF16)
        flipped = mm(perm, block, NT).astype(BF16)
        at = (doc * 2 + parity) * N_SEQ
        for ch in range(CH_OWN):
            base = part * D + ch * N_ALL
            a_ref[at : at + N_SEQ, base : base + N_ALL] = flipped[ch * N_SEQ : (ch + 1) * N_SEQ]
    cos_part = mm(a_ref[:, :D], tc_ref[...], NN)
    sin_part = mm(a_ref[:, D:], ts_ref[...], NN)
    half = D // 2
    sign = jnp.where(
        (lax.broadcasted_iota(jnp.int32, (D, 128), 0) // N_ALL) % 2 == 0, 1.0, -1.0
    ) * (1.0 / math.sqrt(D))
    middle = mm(a_ref[:, :D], sign.astype(BF16), NN)[:, :1]
    mirror = (
        lax.broadcasted_iota(jnp.int32, (half, half), 0)
        + lax.broadcasted_iota(jnp.int32, (half, half), 1)
        == half
    ).astype(BF16)
    low = (cos_part + sin_part).astype(BF16).astype(F32)
    high = mm((cos_part - sin_part).astype(BF16), mirror, NN)
    first = lax.broadcasted_iota(jnp.int32, (ROWS, half), 1) == 0
    high = jnp.where(first, middle.astype(BF16).astype(F32), high)
    mixing = jnp.concatenate([low, high], axis=1)
    residual = jnp.concatenate([x_ref[c].astype(F32) for c in range(N_CHAN)], axis=1)
    normed = norm_rows(residual + mixing, gain_ref[...]).astype(BF16)
    normed_ref[...] = normed
    for out_ref, chunk in zip(out_refs, slot_maps(ids_ref[...])):
        out_ref[...] = mm(chunk, normed, NN).astype(BF16)


def mix_rows(chan_pos, parts, residual, ids, tc, ts, gain):
    return pl.pallas_call(
        mix_kernel,
        out_shape=(
            jax.ShapeDtypeStruct((ROWS, D), BF16),
            *(jax.ShapeDtypeStruct((N_SEQ * count, D), BF16) for _, count in CHUNKS),
        ),
        scratch_shapes=[
            pltpu.VMEM((2, N_ALL * 16, 128), F32),
            pltpu.VMEM((ROWS, 2 * D), BF16),
            pltpu.VMEM((N_CHAN, ROWS, CH), BF16),
        ],
        in_specs=[pl.BlockSpec(memory_space=pltpu.SMEM)]
        + [pl.BlockSpec(memory_space=pltpu.VMEM)] * (5 + N_CHAN),
        compiler_params=kernel_params(24),
        name="mix_rows",
    )(chan_pos, parts, *residual, ids, tc, ts, gain)


def gelu(v):
    inner = math.sqrt(2.0 / math.pi)
    return (0.5 * v) * (1.0 + jnp.tanh(v * (inner + (inner * 0.044715) * (v * v))))


def expert_kernel(x_ref, wi_hbm, wo_hbm, out_ref, wi_ref, wo_ref, h_ref, sem):
    ff = wi_ref.shape[1]
    pieces, block, width = 8, 1024, 256
    step = ff // pieces
    moves = [
        pltpu.make_async_copy(
            wi_hbm.at[0, :, i * step : (i + 1) * step], wi_ref.at[:, i * step : (i + 1) * step], sem.at[i]
        )
        for i in range(pieces)
    ] + [
        pltpu.make_async_copy(
            wo_hbm.at[0, i * step : (i + 1) * step], wo_ref.at[i * step : (i + 1) * step], sem.at[pieces + i]
        )
        for i in range(pieces)
    ]
    for move in moves:
        move.start()
    for i in range(ff // block):
        for j in range(i * block // step, (i + 1) * block // step):
            moves[j].wait()
        cols = slice(i * block, (i + 1) * block)
        h_ref[:, cols] = gelu(mm(x_ref[...], wi_ref[:, cols], NN)).astype(BF16)
    for move in moves[pieces:]:
        move.wait()
    for n in range(D // width):
        cols = slice(n * width, (n + 1) * width)
        out_ref[:, cols] = mm(h_ref[...], wo_ref[:, cols], NN).astype(BF16)


def expert_rows(x, expert_in, expert_out):
    rows, ff = x.shape[0], expert_in.shape[2]
    return pl.pallas_call(
        expert_kernel,
        out_shape=jax.ShapeDtypeStruct((rows, D), BF16),
        in_specs=[pl.BlockSpec(memory_space=pltpu.VMEM)]
        + [pl.BlockSpec(memory_space=pltpu.HBM)] * 2,
        scratch_shapes=[
            pltpu.VMEM((D, ff), BF16),
            pltpu.VMEM((ff, D), BF16),
            pltpu.VMEM((rows, ff), BF16),
            pltpu.SemaphoreType.DMA((16,)),
        ],
        compiler_params=kernel_params(40),
        name="expert_rows",
    )(x, in_hbm(expert_in), in_hbm(expert_out))


def finish_kernel(*refs):
    *back_refs, normed_ref, ids_ref, gain_ref, out_ref = refs
    values = normed_ref[...].astype(F32)
    for back_ref, chunk in zip(back_refs, slot_maps(ids_ref[...])):
        values = values + mm(chunk, back_ref[...], TN)
    out_ref[...] = norm_rows(values, gain_ref[...]).astype(BF16)


def finish_rows(back, normed, ids, gain):
    return pl.pallas_call(
        finish_kernel,
        out_shape=jax.ShapeDtypeStruct((ROWS, D), BF16),
        compiler_params=kernel_params(24),
        name="finish_rows",
    )(*back, normed, ids, gain)


def exchange(x, axes):
    return lax.all_to_all(x, axes, split_axis=0, concat_axis=0, tiled=True)


def local(tokens, routing, expert_in, expert_out, gain_mix, gain_out):
    ids = routing.T.reshape(1, ROWS)
    chan_pos = lax.axis_index("chan").reshape(1)
    tables = [*twiddle_tables(), position_table()]
    cols, rows, tables = split_tokens(
        chan_pos, tokens, *map(jnp.asarray, tables), gain_mix.reshape(1, D), gain_out.reshape(1, D)
    )
    twr, twi, tab, gain_mix, gain_out = tables
    tc, ts = hidden_tables()
    sums = sequence_sums(exchange(cols, SEQ), twr, twi, tab)
    parts = exchange(sums, SEQ_CHAN)
    residual = [rows[0]]
    for i in range(1, N_CHAN):
        ring = [(c, (c + i) % N_CHAN) for c in range(N_CHAN)]
        residual.append(lax.ppermute(rows[i], "chan", ring))
    normed, *outgoing = mix_rows(chan_pos, parts, residual, ids, tc, ts, gain_mix)
    back = []
    for (_, count), x in zip(CHUNKS, outgoing):
        x = exchange(x.reshape(N_SEQ, count, D), SEQ).reshape(N_SEQ * count, D)
        x = expert_rows(x, expert_in, expert_out)
        back.append(exchange(x.reshape(N_SEQ, count, D), SEQ).reshape(N_SEQ * count, D))
    return finish_rows(back, normed, ids, gain_out).reshape(DOCS, QUARTER, D)


def solution(mesh):
    torus = Mesh(
        mesh.devices.reshape(4, 4, 2, mesh.shape["chan"]), ("seq_0", "seq_1", "seq_2", "chan")
    )
    return jax.shard_map(
        local,
        mesh=torus,
        in_specs=(
            P(None, SEQ, "chan"),
            P(SEQ_CHAN, None),
            P(SEQ, None, None),
            P(SEQ, None, None),
            P(),
            P(),
        ),
        out_specs=P(None, SEQ_CHAN, None),
        check_vma=False,
    )
```

```python
import math

import jax
import jax.numpy as jnp
import numpy as np
from jax import lax
from jax.experimental import pallas as pl
from jax.experimental.pallas import tpu as pltpu
from jax.sharding import Mesh
from jax.sharding import PartitionSpec as P

SEQ = ("seq_0", "seq_1", "seq_2")
SEQ_CHAN = ("seq_0", "seq_1", "seq_2", "chan")

D = 1024
L = 8192
DOCS = 4
N_SEQ = 32
N_CHAN = 4
N_ALL = N_SEQ * N_CHAN
POS = L // N_SEQ
CH = D // N_CHAN
QUARTER = POS // N_CHAN
ROWS = DOCS * QUARTER
CH_OWN = CH // N_SEQ
CHUNKS = ((0, 24),)
F32 = jnp.float32
BF16 = jnp.bfloat16
NN = (((1,), (0,)), ((), ()))
NT = (((1,), (1,)), ((), ()))
TN = (((0,), (0,)), ((), ()))


def mm(a, b, dims):
    return lax.dot_general(a, b, dims, preferred_element_type=F32)


def in_hbm(x):
    return pltpu.with_memory_space_constraint(x, pltpu.HBM)


def kernel_params(mib):
    return pltpu.CompilerParams(vmem_limit_bytes=mib << 20)


def twiddle_tables():
    k = np.arange(N_SEQ)[:, None]
    j = np.arange(POS)[None, :]
    angle = 2.0 * np.pi * ((k * j) % L) / L
    scale = 1.0 / math.sqrt(L)
    return (
        (np.cos(angle) * scale).astype(np.float32),
        (-np.sin(angle) * scale).astype(np.float32),
    )


def position_table():
    j = np.arange(POS)
    m = (np.arange(2)[:, None] + 2 * np.arange(POS // 2)[None, :]).reshape(-1)
    angle = 2.0 * np.pi * ((m[:, None] * j[None, :]) % POS) / POS
    cos, sin = np.cos(angle), np.sin(angle)
    return np.concatenate(
        [np.concatenate([cos, sin], 1), np.concatenate([sin, -cos], 1)], 0
    ).astype(BF16)


def tables_kernel(tc_ref, ts_ref):
    block = 128
    f = lax.broadcasted_iota(jnp.int32, (block, D // 2), 1)
    for i in range(D // block):
        row = lax.broadcasted_iota(jnp.int32, (block, D // 2), 0) + i * block
        ch, owner = row // N_ALL, row % N_ALL
        d = owner % N_CHAN * CH + owner // N_CHAN * CH_OWN + ch
        turn = (d * f) % D
        turn = jnp.where(turn >= D // 2, turn - D, turn)
        angle = turn.astype(F32) * (2.0 * math.pi / D)
        factor = 1.0 / math.sqrt(D)
        rows = slice(i * block, (i + 1) * block)
        tc_ref[rows, :] = (jnp.cos(angle) * factor).astype(BF16)
        ts_ref[rows, :] = (-jnp.sin(angle) * factor).astype(BF16)


def hidden_tables():
    return pl.pallas_call(
        tables_kernel,
        out_shape=(jax.ShapeDtypeStruct((D, D // 2), BF16),) * 2,
        compiler_params=kernel_params(8),
        name="hidden_tables",
    )()


def split_kernel(chan_ref, tok_hbm, col_ref, *refs):
    *row_refs, tok_ref, sem = refs
    moves = [
        pltpu.make_async_copy(tok_hbm.at[doc], tok_ref.at[doc], sem.at[doc]) for doc in range(DOCS)
    ]
    for move in moves:
        move.start()
    eye = (
        lax.broadcasted_iota(jnp.int32, (CH, CH), 0)
        == lax.broadcasted_iota(jnp.int32, (CH, CH), 1)
    ).astype(BF16)
    for pair in range(DOCS // 2):
        flipped = []
        for doc in (2 * pair, 2 * pair + 1):
            moves[doc].wait()
            flipped.append(mm(eye, tok_ref[doc], NT).reshape(N_SEQ, CH_OWN, POS))
        both = jnp.concatenate(flipped, axis=1).astype(BF16)
        col_ref[:, 2 * CH_OWN * pair : 2 * CH_OWN * (pair + 1), :] = both
    for i, row_ref in enumerate(row_refs):
        first = pl.multiple_of((chan_ref[0] + i + 1) % N_CHAN * QUARTER, QUARTER)
        for doc in range(DOCS):
            row_ref[doc * QUARTER : (doc + 1) * QUARTER, :] = tok_ref[
                doc, pl.ds(first, QUARTER), :
            ]


def split_tokens(chan_pos, tokens):
    cols, *rows = pl.pallas_call(
        split_kernel,
        out_shape=(
            jax.ShapeDtypeStruct((N_SEQ, DOCS * CH_OWN, POS), BF16),
            *(jax.ShapeDtypeStruct((ROWS, CH), BF16) for _ in range(N_CHAN - 1)),
        ),
        in_specs=[
            pl.BlockSpec(memory_space=pltpu.SMEM),
            pl.BlockSpec(memory_space=pltpu.HBM),
        ],
        scratch_shapes=[
            pltpu.VMEM((DOCS, POS, CH), BF16),
            pltpu.SemaphoreType.DMA((DOCS,)),
        ],
        compiler_params=kernel_params(8),
        name="split_tokens",
    )(chan_pos, in_hbm(tokens))
    return cols, rows


def bring_kernel(*refs):
    n = (len(refs) - 1) // 2
    moves = [pltpu.make_async_copy(refs[i], refs[n + i], refs[-1].at[i]) for i in range(n)]
    for move in moves:
        move.start()
    for move in moves:
        move.wait()


def bring(*arrays):
    return pl.pallas_call(
        bring_kernel,
        out_shape=tuple(jax.ShapeDtypeStruct(t.shape, t.dtype) for t in arrays),
        in_specs=[pl.BlockSpec(memory_space=pltpu.HBM)] * len(arrays),
        scratch_shapes=[pltpu.SemaphoreType.DMA((len(arrays),))],
        compiler_params=kernel_params(4),
        name="bring",
    )(*map(in_hbm, arrays))


def real_fft(x):
    n = len(x)
    if n == 1:
        return [(x[0], None)]
    even = real_fft(x[0::2])
    odd = real_fft(x[1::2])
    if n == 2:
        return [(even[0][0] + odd[0][0], None), (even[0][0] - odd[0][0], None)]
    out = [None] * (n // 2 + 1)
    for k in range(n // 4 + 1):
        er, ei = even[k]
        orr, oi = odd[k]
        if k == 0:
            out[0] = (er + orr, None)
            out[n // 2] = (er - orr, None)
        elif 4 * k == n:
            out[k] = (er, -orr)
        else:
            c = math.cos(2.0 * math.pi * k / n)
            s = -math.sin(2.0 * math.pi * k / n)
            if 8 * k == n:
                tr, ti = (orr + oi) * c, (oi - orr) * c
            else:
                tr, ti = orr * c - oi * s, orr * s + oi * c
            out[k] = (er + tr, ei + ti)
            out[n // 2 - k] = (er - tr, ti - ei)
    return out


def sequence_kernel(x_ref, twr_ref, twi_ref, tab_ref, out_ref, t_ref, s_ref):
    for doc in range(DOCS):
        for half in range(POS // 128):
            lanes = slice(half * 128, (half + 1) * 128)
            lanes_im = slice(POS + half * 128, POS + (half + 1) * 128)
            rows = slice(doc * CH_OWN, (doc + 1) * CH_OWN)
            freq = real_fft([x_ref[s, rows, lanes].astype(F32) for s in range(N_SEQ)])
            for k in range(N_SEQ):
                if k <= N_SEQ // 2:
                    fr, fi = freq[k]
                else:
                    fr, fi = freq[N_SEQ - k]
                    fi = -fi
                wr = twr_ref[k : k + 1, lanes]
                wi = twi_ref[k : k + 1, lanes]
                if fi is None:
                    tr, ti = fr * wr, fr * wi
                else:
                    tr, ti = fr * wr - fi * wi, fr * wi + fi * wr
                t_ref[doc, k * CH_OWN : (k + 1) * CH_OWN, lanes] = tr
                t_ref[doc, k * CH_OWN : (k + 1) * CH_OWN, lanes_im] = ti
    for doc in range(DOCS):
        part = mm(tab_ref[...], t_ref[doc].astype(BF16), NT)
        for i in range(4):
            for h in range(2):
                s_ref[h, pl.ds(4 * i + doc, N_ALL, stride=16), :] = part[
                    i * N_ALL : (i + 1) * N_ALL, h * 128 : (h + 1) * 128
                ]
    for h in range(2):
        out_ref[:, :, h * 128 : (h + 1) * 128] = s_ref[h].reshape(N_ALL, 16, 128).astype(BF16)


def sequence_sums(cols, twr, twi, tab):
    return pl.pallas_call(
        sequence_kernel,
        out_shape=jax.ShapeDtypeStruct((N_ALL, 16, N_SEQ * CH_OWN), BF16),
        scratch_shapes=[
            pltpu.VMEM((DOCS, N_SEQ * CH_OWN, 2 * POS), F32),
            pltpu.VMEM((2, N_ALL * 16, 128), F32),
        ],
        compiler_params=kernel_params(24),
        name="sequence_sums",
    )(cols, twr, twi, tab)


def norm_rows(values, gain):
    center = values - jnp.mean(values, axis=-1, keepdims=True)
    spread = jnp.mean(center * center, axis=-1, keepdims=True)
    return center * lax.rsqrt(spread + 1e-05) * gain


def slot_maps(ids):
    one = (lax.broadcasted_iota(jnp.int32, (N_SEQ, ROWS), 0) == ids).astype(F32)
    earlier = (
        lax.broadcasted_iota(jnp.int32, (ROWS, ROWS), 0)
        < lax.broadcasted_iota(jnp.int32, (ROWS, ROWS), 1)
    ).astype(BF16)
    before = mm(one.astype(BF16), earlier, NN)
    rank = jnp.sum(before * one, axis=0, keepdims=True).astype(jnp.int32)
    maps = []
    for start, count in CHUNKS:
        inside = (rank >= start) & (rank < start + count)
        target = jnp.where(inside, ids * count + rank - start, -1)
        slots = lax.broadcasted_iota(jnp.int32, (N_SEQ * count, ROWS), 0)
        maps.append((slots == target).astype(BF16))
    return maps


def mix_kernel(chan_ref, r_ref, tok_hbm, *refs):
    res_refs, rest = refs[: N_CHAN - 1], refs[N_CHAN - 1 :]
    ids_ref, tc_ref, ts_ref, gain_ref, normed_ref, *out_refs, s_ref, a_ref, x_ref, sem = rest
    chan = chan_ref[0]
    first = pl.multiple_of(chan * QUARTER, QUARTER)
    moves = [
        pltpu.make_async_copy(
            tok_hbm.at[doc, pl.ds(first, QUARTER), :],
            x_ref.at[chan, pl.ds(doc * QUARTER, QUARTER), :],
            sem.at[N_CHAN - 1 + doc],
        )
        for doc in range(DOCS)
    ] + [
        pltpu.make_async_copy(res_ref, x_ref.at[(chan + N_CHAN - 1 - i) % N_CHAN], sem.at[i])
        for i, res_ref in enumerate(res_refs)
    ]
    for move in moves:
        move.start()
    lanes = N_SEQ * CH_OWN
    for h in range(2):
        s_ref[h] = r_ref[:, :, h * 128 : (h + 1) * 128].astype(F32).reshape(N_ALL * 16, 128)
    row = lax.broadcasted_iota(jnp.int32, (lanes, lanes), 0)
    col = lax.broadcasted_iota(jnp.int32, (lanes, lanes), 1)
    perm = ((row % N_SEQ == col // CH_OWN) & (row // N_SEQ == col % CH_OWN)).astype(BF16)
    for r in range(16):
        part, parity, doc = r // 8, (r // 4) % 2, r % 4
        block = jnp.concatenate(
            [s_ref[h, pl.ds(r, N_ALL, stride=16), :] for h in range(2)], axis=1
        ).astype(BF16)
        flipped = mm(perm, block, NT).astype(BF16)
        at = (doc * 2 + parity) * N_SEQ
        for ch in range(CH_OWN):
            base = part * D + ch * N_ALL
            a_ref[at : at + N_SEQ, base : base + N_ALL] = flipped[ch * N_SEQ : (ch + 1) * N_SEQ]
    cos_part = mm(a_ref[:, :D], tc_ref[...], NN)
    sin_part = mm(a_ref[:, D:], ts_ref[...], NN)
    half = D // 2
    sign = jnp.where(
        (lax.broadcasted_iota(jnp.int32, (D, 128), 0) // N_ALL) % 2 == 0, 1.0, -1.0
    ) * (1.0 / math.sqrt(D))
    middle = mm(a_ref[:, :D], sign.astype(BF16), NN)[:, :1]
    mirror = (
        lax.broadcasted_iota(jnp.int32, (half, half), 0)
        + lax.broadcasted_iota(jnp.int32, (half, half), 1)
        == half
    ).astype(BF16)
    low = (cos_part + sin_part).astype(BF16).astype(F32)
    high = mm((cos_part - sin_part).astype(BF16), mirror, NN)
    first = lax.broadcasted_iota(jnp.int32, (ROWS, half), 1) == 0
    high = jnp.where(first, middle.astype(BF16).astype(F32), high)
    mixing = jnp.concatenate([low, high], axis=1)
    for move in moves:
        move.wait()
    residual = jnp.concatenate([x_ref[c].astype(F32) for c in range(N_CHAN)], axis=1)
    normed = norm_rows(residual + mixing, gain_ref[...]).astype(BF16)
    normed_ref[...] = normed
    for out_ref, chunk in zip(out_refs, slot_maps(ids_ref[...])):
        out_ref[...] = mm(chunk, normed, NN).astype(BF16)


def mix_rows(chan_pos, parts, tokens, residual, ids, tc, ts, gain):
    return pl.pallas_call(
        mix_kernel,
        out_shape=(
            jax.ShapeDtypeStruct((ROWS, D), BF16),
            *(jax.ShapeDtypeStruct((N_SEQ * count, D), BF16) for _, count in CHUNKS),
        ),
        scratch_shapes=[
            pltpu.VMEM((2, N_ALL * 16, 128), F32),
            pltpu.VMEM((ROWS, 2 * D), BF16),
            pltpu.VMEM((N_CHAN, ROWS, CH), BF16),
            pltpu.SemaphoreType.DMA((N_CHAN - 1 + DOCS,)),
        ],
        in_specs=[pl.BlockSpec(memory_space=pltpu.SMEM), pl.BlockSpec(memory_space=pltpu.VMEM)]
        + [pl.BlockSpec(memory_space=pltpu.HBM)] * N_CHAN
        + [pl.BlockSpec(memory_space=pltpu.VMEM)] * 4,
        compiler_params=kernel_params(24),
        name="mix_rows",
    )(chan_pos, parts, *map(in_hbm, (tokens, *residual)), ids, tc, ts, gain)


def gelu(v):
    inner = math.sqrt(2.0 / math.pi)
    return (0.5 * v) * (1.0 + jnp.tanh(v * (inner + (inner * 0.044715) * (v * v))))


def expert_kernel(x_ref, wi_hbm, wo_hbm, out_ref, wi_ref, wo_ref, h_ref, sem):
    ff = wi_ref.shape[1]
    pieces, block, width = 8, 1024, 256
    step = ff // pieces
    moves = [
        pltpu.make_async_copy(
            wi_hbm.at[0, :, i * step : (i + 1) * step], wi_ref.at[:, i * step : (i + 1) * step], sem.at[i]
        )
        for i in range(pieces)
    ] + [
        pltpu.make_async_copy(
            wo_hbm.at[0, i * step : (i + 1) * step], wo_ref.at[i * step : (i + 1) * step], sem.at[pieces + i]
        )
        for i in range(pieces)
    ]
    for move in moves:
        move.start()
    for i in range(ff // block):
        for j in range(i * block // step, (i + 1) * block // step):
            moves[j].wait()
        cols = slice(i * block, (i + 1) * block)
        h_ref[:, cols] = gelu(mm(x_ref[...], wi_ref[:, cols], NN)).astype(BF16)
    for move in moves[pieces:]:
        move.wait()
    for n in range(D // width):
        cols = slice(n * width, (n + 1) * width)
        out_ref[:, cols] = mm(h_ref[...], wo_ref[:, cols], NN).astype(BF16)


def expert_rows(x, expert_in, expert_out):
    rows, ff = x.shape[0], expert_in.shape[2]
    return pl.pallas_call(
        expert_kernel,
        out_shape=jax.ShapeDtypeStruct((rows, D), BF16),
        in_specs=[pl.BlockSpec(memory_space=pltpu.VMEM)]
        + [pl.BlockSpec(memory_space=pltpu.HBM)] * 2,
        scratch_shapes=[
            pltpu.VMEM((D, ff), BF16),
            pltpu.VMEM((ff, D), BF16),
            pltpu.VMEM((rows, ff), BF16),
            pltpu.SemaphoreType.DMA((16,)),
        ],
        compiler_params=kernel_params(40),
        name="expert_rows",
    )(x, in_hbm(expert_in), in_hbm(expert_out))


def finish_kernel(*refs):
    *back_refs, normed_ref, ids_ref, gain_ref, out_ref = refs
    values = normed_ref[...].astype(F32)
    for back_ref, chunk in zip(back_refs, slot_maps(ids_ref[...])):
        values = values + mm(chunk, back_ref[...], TN)
    out_ref[...] = norm_rows(values, gain_ref[...]).astype(BF16)


def finish_rows(back, normed, ids, gain):
    return pl.pallas_call(
        finish_kernel,
        out_shape=jax.ShapeDtypeStruct((ROWS, D), BF16),
        compiler_params=kernel_params(24),
        name="finish_rows",
    )(*back, normed, ids, gain)


def exchange(x, axes):
    return lax.all_to_all(x, axes, split_axis=0, concat_axis=0, tiled=True)


def local(tokens, routing, expert_in, expert_out, gain_mix, gain_out):
    ids = routing.T.reshape(1, ROWS)
    chan_pos = lax.axis_index("chan").reshape(1)
    cols, rows = split_tokens(chan_pos, tokens)
    tables = [jnp.asarray(t) for t in (*twiddle_tables(), position_table())]
    twr, twi, tab, gain_mix, gain_out = bring(
        *tables, gain_mix.reshape(1, D), gain_out.reshape(1, D)
    )
    tc, ts = hidden_tables()
    sums = sequence_sums(exchange(cols, SEQ), twr, twi, tab)
    parts = exchange(sums, SEQ_CHAN)
    residual = []
    for i in range(1, N_CHAN):
        ring = [(c, (c + i) % N_CHAN) for c in range(N_CHAN)]
        residual.append(lax.ppermute(rows[i - 1], "chan", ring))
    normed, *outgoing = mix_rows(chan_pos, parts, tokens, residual, ids, tc, ts, gain_mix)
    back = []
    for (_, count), x in zip(CHUNKS, outgoing):
        x = exchange(x.reshape(N_SEQ, count, D), SEQ).reshape(N_SEQ * count, D)
        x = expert_rows(x, expert_in, expert_out)
        back.append(exchange(x.reshape(N_SEQ, count, D), SEQ).reshape(N_SEQ * count, D))
    return finish_rows(back, normed, ids, gain_out).reshape(DOCS, QUARTER, D)


def solution(mesh):
    torus = Mesh(
        mesh.devices.reshape(4, 4, 2, mesh.shape["chan"]), ("seq_0", "seq_1", "seq_2", "chan")
    )
    return jax.shard_map(
        local,
        mesh=torus,
        in_specs=(
            P(None, SEQ, "chan"),
            P(SEQ_CHAN, None),
            P(SEQ, None, None),
            P(SEQ, None, None),
            P(),
            P(),
        ),
        out_specs=P(None, SEQ_CHAN, None),
        check_vma=False,
    )
```

```python
import math

import jax
import jax.numpy as jnp
import numpy as np
from jax import lax
from jax.experimental import pallas as pl
from jax.experimental.pallas import tpu as pltpu
from jax.sharding import Mesh
from jax.sharding import PartitionSpec as P

SEQ = ("seq_0", "seq_1", "seq_2")
SEQ_CHAN = ("seq_0", "seq_1", "seq_2", "chan")

D = 1024
L = 8192
DOCS = 4
N_SEQ = 32
N_CHAN = 4
N_ALL = N_SEQ * N_CHAN
POS = L // N_SEQ
CH = D // N_CHAN
QUARTER = POS // N_CHAN
ROWS = DOCS * QUARTER
CH_OWN = CH // N_ALL
LANES = N_SEQ * DOCS * CH_OWN
PARTS = 8
CHUNKS = ((0, 24),)
F32 = jnp.float32
BF16 = jnp.bfloat16
NN = (((1,), (0,)), ((), ()))
NT = (((1,), (1,)), ((), ()))
TN = (((0,), (0,)), ((), ()))


def mm(a, b, dims):
    return lax.dot_general(a, b, dims, preferred_element_type=F32)


def in_hbm(x):
    return pltpu.with_memory_space_constraint(x, pltpu.HBM)


def kernel_params(mib):
    return pltpu.CompilerParams(vmem_limit_bytes=mib << 20)


def twiddle_tables():
    k = np.arange(N_SEQ)[:, None]
    j = np.arange(POS)[None, :]
    angle = 2.0 * np.pi * ((k * j) % L) / L
    scale = 1.0 / math.sqrt(L)
    return (
        (np.cos(angle) * scale).astype(np.float32),
        (-np.sin(angle) * scale).astype(np.float32),
    )


def position_table():
    j = np.arange(POS)
    m = (np.arange(2)[:, None] + 2 * np.arange(POS // 2)[None, :]).reshape(-1)
    angle = 2.0 * np.pi * ((m[:, None] * j[None, :]) % POS) / POS
    cos, sin = np.cos(angle), np.sin(angle)
    return np.concatenate(
        [np.concatenate([cos, sin], 1), np.concatenate([sin, -cos], 1)], 0
    ).astype(BF16)


def tables_kernel(tc_ref, ts_ref):
    block = 128
    f = lax.broadcasted_iota(jnp.int32, (block, D // 2), 1)
    for i in range(D // 2 // block):
        owner = lax.broadcasted_iota(jnp.int32, (block, D // 2), 0)
        d = i // CH_OWN * CH + CH_OWN * owner + i % CH_OWN
        turn = (d * f) % D
        turn = jnp.where(turn >= D // 2, turn - D, turn)
        angle = turn.astype(F32) * (2.0 * math.pi / D)
        factor = 1.0 / math.sqrt(D)
        rows = slice(i * block, (i + 1) * block)
        tc_ref[rows, :] = (jnp.cos(angle) * factor).astype(BF16)
        ts_ref[rows, :] = (-jnp.sin(angle) * factor).astype(BF16)


def hidden_tables():
    return pl.pallas_call(
        tables_kernel,
        out_shape=(jax.ShapeDtypeStruct((D // 2, D // 2), BF16),) * 2,
        compiler_params=kernel_params(8),
        name="hidden_tables",
    )()


def split_kernel(chan_ref, tok_hbm, col_ref, *refs):
    *row_refs, tok_ref, s_ref, sem = refs
    moves = [
        pltpu.make_async_copy(tok_hbm.at[doc], tok_ref.at[doc], sem.at[doc]) for doc in range(DOCS)
    ]
    for move in moves:
        move.start()
    row = lax.broadcasted_iota(jnp.int32, (CH, CH), 0)
    index = CH_OWN * (row % N_ALL) + row // N_ALL
    index = jnp.where(chan_ref[0] < N_CHAN // 2, index, (CH - index) % CH)
    pick = (lax.broadcasted_iota(jnp.int32, (CH, CH), 1) == index).astype(BF16)
    for doc in range(DOCS):
        moves[doc].wait()
        flipped = mm(pick, tok_ref[doc], NT)
        for j in range(CH_OWN):
            for h in range(POS // 128):
                s_ref[h, pl.ds(doc * CH_OWN + j, N_ALL, stride=PARTS), :] = flipped[
                    j * N_ALL : (j + 1) * N_ALL, h * 128 : (h + 1) * 128
                ]
    for h in range(POS // 128):
        col_ref[:, :, h * 128 : (h + 1) * 128] = (
            s_ref[h].reshape(N_ALL, PARTS, 128).astype(BF16)
        )
    for i, row_ref in enumerate(row_refs):
        first = pl.multiple_of((chan_ref[0] + i + 1) % N_CHAN * QUARTER, QUARTER)
        for doc in range(DOCS):
            row_ref[doc * QUARTER : (doc + 1) * QUARTER, :] = tok_ref[
                doc, pl.ds(first, QUARTER), :
            ]


def split_tokens(chan_pos, tokens):
    cols, *rows = pl.pallas_call(
        split_kernel,
        out_shape=(
            jax.ShapeDtypeStruct((N_ALL, PARTS, POS), BF16),
            *(jax.ShapeDtypeStruct((ROWS, CH), BF16) for _ in range(N_CHAN - 1)),
        ),
        in_specs=[
            pl.BlockSpec(memory_space=pltpu.SMEM),
            pl.BlockSpec(memory_space=pltpu.HBM),
        ],
        scratch_shapes=[
            pltpu.VMEM((DOCS, POS, CH), BF16),
            pltpu.VMEM((POS // 128, N_ALL * PARTS, 128), F32),
            pltpu.SemaphoreType.DMA((DOCS,)),
        ],
        compiler_params=kernel_params(8),
        name="split_tokens",
    )(chan_pos, in_hbm(tokens))
    return cols, rows


def bring_kernel(*refs):
    n = (len(refs) - 1) // 2
    moves = [pltpu.make_async_copy(refs[i], refs[n + i], refs[-1].at[i]) for i in range(n)]
    for move in moves:
        move.start()
    for move in moves:
        move.wait()


def bring(*arrays):
    return pl.pallas_call(
        bring_kernel,
        out_shape=tuple(jax.ShapeDtypeStruct(t.shape, t.dtype) for t in arrays),
        in_specs=[pl.BlockSpec(memory_space=pltpu.HBM)] * len(arrays),
        scratch_shapes=[pltpu.SemaphoreType.DMA((len(arrays),))],
        compiler_params=kernel_params(4),
        name="bring",
    )(*map(in_hbm, arrays))


def real_fft(x):
    n = len(x)
    if n == 1:
        return [(x[0], None)]
    even = real_fft(x[0::2])
    odd = real_fft(x[1::2])
    if n == 2:
        return [(even[0][0] + odd[0][0], None), (even[0][0] - odd[0][0], None)]
    out = [None] * (n // 2 + 1)
    for k in range(n // 4 + 1):
        er, ei = even[k]
        orr, oi = odd[k]
        if k == 0:
            out[0] = (er + orr, None)
            out[n // 2] = (er - orr, None)
        elif 4 * k == n:
            out[k] = (er, -orr)
        else:
            c = math.cos(2.0 * math.pi * k / n)
            s = -math.sin(2.0 * math.pi * k / n)
            if 8 * k == n:
                tr, ti = (orr + oi) * c, (oi - orr) * c
            else:
                tr, ti = orr * c - oi * s, orr * s + oi * c
            out[k] = (er + tr, ei + ti)
            out[n // 2 - k] = (er - tr, ti - ei)
    return out


def sequence_kernel(owner_ref, x_ref, twr_ref, twi_ref, tab_ref, out_ref, t_ref, s_ref):
    rows = DOCS * CH_OWN
    own_mirror = (lax.broadcasted_iota(jnp.int32, (rows, 128), 0) % CH_OWN == 0) & (
        owner_ref[0] == 0
    )

    def folded(g, s, lanes):
        third = x_ref[N_CHAN * s + 2, :, lanes].astype(F32)
        fourth = x_ref[N_CHAN * s + 3, :, lanes].astype(F32)
        base = x_ref[N_CHAN * s + g // 2, :, lanes].astype(F32)
        if g == 0:
            return base + jnp.where(own_mirror, 0.0, fourth)
        if g == 1:
            return jnp.where(own_mirror, third, base - fourth)
        other = jnp.where(own_mirror, fourth, third)
        return base + other if g == 2 else base - other

    for g in range(4):
        for half in range(POS // 128):
            lanes = slice(half * 128, (half + 1) * 128)
            lanes_im = slice(POS + half * 128, POS + (half + 1) * 128)
            freq = real_fft([folded(g, s, lanes) for s in range(N_SEQ)])
            for k in range(N_SEQ):
                if k <= N_SEQ // 2:
                    fr, fi = freq[k]
                else:
                    fr, fi = freq[N_SEQ - k]
                    fi = -fi
                wr = twr_ref[k : k + 1, lanes]
                wi = twi_ref[k : k + 1, lanes]
                if fi is None:
                    tr, ti = fr * wr, fr * wi
                else:
                    tr, ti = fr * wr - fi * wi, fr * wi + fi * wr
                if g == 1:
                    tr, ti = jnp.where(own_mirror, ti, tr), jnp.where(own_mirror, -tr, ti)
                t_ref[g, k * rows : (k + 1) * rows, lanes] = tr
                t_ref[g, k * rows : (k + 1) * rows, lanes_im] = ti
    for g in range(4):
        kind = slice(g % 2 * POS, (g % 2 + 1) * POS)
        part = mm(tab_ref[kind, :], t_ref[g].astype(BF16), NT)
        for parity in range(2):
            for h in range(LANES // 128):
                s_ref[h, pl.ds(2 * g + parity, N_ALL, stride=PARTS), :] = part[
                    parity * N_ALL : (parity + 1) * N_ALL, h * 128 : (h + 1) * 128
                ]
    for h in range(LANES // 128):
        out_ref[:, :, h * 128 : (h + 1) * 128] = (
            s_ref[h].reshape(N_ALL, PARTS, 128).astype(BF16)
        )


def sequence_sums(owner, cols, twr, twi, tab):
    return pl.pallas_call(
        sequence_kernel,
        out_shape=jax.ShapeDtypeStruct((N_ALL, PARTS, LANES), BF16),
        in_specs=[pl.BlockSpec(memory_space=pltpu.SMEM)]
        + [pl.BlockSpec(memory_space=pltpu.VMEM)] * 4,
        scratch_shapes=[
            pltpu.VMEM((4, LANES, 2 * POS), F32),
            pltpu.VMEM((LANES // 128, N_ALL * PARTS, 128), F32),
        ],
        compiler_params=kernel_params(24),
        name="sequence_sums",
    )(owner, cols, twr, twi, tab)


def norm_rows(values, gain):
    center = values - jnp.mean(values, axis=-1, keepdims=True)
    spread = jnp.mean(center * center, axis=-1, keepdims=True)
    return center * lax.rsqrt(spread + 1e-05) * gain


def slot_maps(ids):
    one = (lax.broadcasted_iota(jnp.int32, (N_SEQ, ROWS), 0) == ids).astype(F32)
    earlier = (
        lax.broadcasted_iota(jnp.int32, (ROWS, ROWS), 0)
        < lax.broadcasted_iota(jnp.int32, (ROWS, ROWS), 1)
    ).astype(BF16)
    before = mm(one.astype(BF16), earlier, NN)
    rank = jnp.sum(before * one, axis=0, keepdims=True).astype(jnp.int32)
    maps = []
    for start, count in CHUNKS:
        inside = (rank >= start) & (rank < start + count)
        target = jnp.where(inside, ids * count + rank - start, -1)
        slots = lax.broadcasted_iota(jnp.int32, (N_SEQ * count, ROWS), 0)
        maps.append((slots == target).astype(BF16))
    return maps


def mix_kernel(chan_ref, r_ref, tok_hbm, *refs):
    res_refs, rest = refs[: N_CHAN - 1], refs[N_CHAN - 1 :]
    ids_ref, tc_ref, ts_ref, gain_ref, normed_ref, *out_refs, s_ref, a_ref, x_ref, sem = rest
    chan = chan_ref[0]
    first = pl.multiple_of(chan * QUARTER, QUARTER)
    moves = [
        pltpu.make_async_copy(
            tok_hbm.at[doc, pl.ds(first, QUARTER), :],
            x_ref.at[chan, pl.ds(doc * QUARTER, QUARTER), :],
            sem.at[N_CHAN - 1 + doc],
        )
        for doc in range(DOCS)
    ] + [
        pltpu.make_async_copy(res_ref, x_ref.at[(chan + N_CHAN - 1 - i) % N_CHAN], sem.at[i])
        for i, res_ref in enumerate(res_refs)
    ]
    for move in moves:
        move.start()
    for h in range(LANES // 128):
        s_ref[h] = r_ref[:, :, h * 128 : (h + 1) * 128].astype(F32).reshape(N_ALL * PARTS, 128)
    row = lax.broadcasted_iota(jnp.int32, (LANES, LANES), 0)
    at = row % N_SEQ * (DOCS * CH_OWN) + row // N_SEQ % DOCS * CH_OWN + row // (N_SEQ * DOCS)
    perm = (lax.broadcasted_iota(jnp.int32, (LANES, LANES), 1) == at).astype(BF16)
    half = D // 2
    for r in range(PARTS):
        g, parity = r // 2, r % 2
        block = jnp.concatenate(
            [s_ref[h, pl.ds(r, N_ALL, stride=PARTS), :] for h in range(LANES // 128)], axis=1
        ).astype(BF16)
        flipped = mm(perm, block, NT).astype(BF16)
        for j in range(CH_OWN):
            base = g % 2 * half + g // 2 * CH + j * N_ALL
            for doc in range(DOCS):
                first = (doc * 2 + parity) * N_SEQ
                start = (j * DOCS + doc) * N_SEQ
                a_ref[first : first + N_SEQ, base : base + N_ALL] = flipped[start : start + N_SEQ]
    factor = 1.0 / math.sqrt(D)
    own = a_ref[:, half : half + 1].astype(F32) * factor
    swing = 1.0 - 2.0 * (lax.broadcasted_iota(jnp.int32, (ROWS, half), 1) % 2).astype(F32)
    cos_part = mm(a_ref[:, :half], tc_ref[...], NN) + own * swing
    sin_part = mm(a_ref[:, half:], ts_ref[...], NN)
    sign = jnp.where(
        lax.broadcasted_iota(jnp.int32, (half, 128), 0) // N_ALL % CH_OWN == 0, factor, -factor
    )
    middle = mm(a_ref[:, :half], sign.astype(BF16), NN)[:, :1] + own
    mirror = (
        lax.broadcasted_iota(jnp.int32, (half, half), 0)
        + lax.broadcasted_iota(jnp.int32, (half, half), 1)
        == half
    ).astype(BF16)
    low = (cos_part + sin_part).astype(BF16).astype(F32)
    high = mm((cos_part - sin_part).astype(BF16), mirror, NN)
    first = lax.broadcasted_iota(jnp.int32, (ROWS, half), 1) == 0
    high = jnp.where(first, middle.astype(BF16).astype(F32), high)
    mixing = jnp.concatenate([low, high], axis=1)
    for move in moves:
        move.wait()
    residual = jnp.concatenate([x_ref[c].astype(F32) for c in range(N_CHAN)], axis=1)
    normed = norm_rows(residual + mixing, gain_ref[...]).astype(BF16)
    normed_ref[...] = normed
    for out_ref, chunk in zip(out_refs, slot_maps(ids_ref[...])):
        out_ref[...] = mm(chunk, normed, NN).astype(BF16)


def mix_rows(chan_pos, parts, tokens, residual, ids, tc, ts, gain):
    return pl.pallas_call(
        mix_kernel,
        out_shape=(
            jax.ShapeDtypeStruct((ROWS, D), BF16),
            *(jax.ShapeDtypeStruct((N_SEQ * count, D), BF16) for _, count in CHUNKS),
        ),
        scratch_shapes=[
            pltpu.VMEM((LANES // 128, N_ALL * PARTS, 128), F32),
            pltpu.VMEM((ROWS, D), BF16),
            pltpu.VMEM((N_CHAN, ROWS, CH), BF16),
            pltpu.SemaphoreType.DMA((N_CHAN - 1 + DOCS,)),
        ],
        in_specs=[pl.BlockSpec(memory_space=pltpu.SMEM), pl.BlockSpec(memory_space=pltpu.VMEM)]
        + [pl.BlockSpec(memory_space=pltpu.HBM)] * N_CHAN
        + [pl.BlockSpec(memory_space=pltpu.VMEM)] * 4,
        compiler_params=kernel_params(24),
        name="mix_rows",
    )(chan_pos, parts, *map(in_hbm, (tokens, *residual)), ids, tc, ts, gain)


def gelu(v):
    inner = math.sqrt(2.0 / math.pi)
    return (0.5 * v) * (1.0 + jnp.tanh(v * (inner + (inner * 0.044715) * (v * v))))


def expert_kernel(x_ref, wi_hbm, wo_hbm, out_ref, wi_ref, wo_ref, h_ref, sem):
    ff = wi_ref.shape[1]
    pieces, block, width = 8, 1024, 256
    step = ff // pieces
    moves = [
        pltpu.make_async_copy(
            wi_hbm.at[0, :, i * step : (i + 1) * step], wi_ref.at[:, i * step : (i + 1) * step], sem.at[i]
        )
        for i in range(pieces)
    ] + [
        pltpu.make_async_copy(
            wo_hbm.at[0, i * step : (i + 1) * step], wo_ref.at[i * step : (i + 1) * step], sem.at[pieces + i]
        )
        for i in range(pieces)
    ]
    for move in moves:
        move.start()
    for i in range(ff // block):
        for j in range(i * block // step, (i + 1) * block // step):
            moves[j].wait()
        cols = slice(i * block, (i + 1) * block)
        h_ref[:, cols] = gelu(mm(x_ref[...], wi_ref[:, cols], NN)).astype(BF16)
    for move in moves[pieces:]:
        move.wait()
    for n in range(D // width):
        cols = slice(n * width, (n + 1) * width)
        out_ref[:, cols] = mm(h_ref[...], wo_ref[:, cols], NN).astype(BF16)


def expert_rows(x, expert_in, expert_out):
    rows, ff = x.shape[0], expert_in.shape[2]
    return pl.pallas_call(
        expert_kernel,
        out_shape=jax.ShapeDtypeStruct((rows, D), BF16),
        in_specs=[pl.BlockSpec(memory_space=pltpu.VMEM)]
        + [pl.BlockSpec(memory_space=pltpu.HBM)] * 2,
        scratch_shapes=[
            pltpu.VMEM((D, ff), BF16),
            pltpu.VMEM((ff, D), BF16),
            pltpu.VMEM((rows, ff), BF16),
            pltpu.SemaphoreType.DMA((16,)),
        ],
        compiler_params=kernel_params(40),
        name="expert_rows",
    )(x, in_hbm(expert_in), in_hbm(expert_out))


def finish_kernel(*refs):
    *back_refs, normed_ref, ids_ref, gain_ref, out_ref = refs
    values = normed_ref[...].astype(F32)
    for back_ref, chunk in zip(back_refs, slot_maps(ids_ref[...])):
        values = values + mm(chunk, back_ref[...], TN)
    out_ref[...] = norm_rows(values, gain_ref[...]).astype(BF16)


def finish_rows(back, normed, ids, gain):
    return pl.pallas_call(
        finish_kernel,
        out_shape=jax.ShapeDtypeStruct((ROWS, D), BF16),
        compiler_params=kernel_params(24),
        name="finish_rows",
    )(*back, normed, ids, gain)


def exchange(x, axes):
    return lax.all_to_all(x, axes, split_axis=0, concat_axis=0, tiled=True)


def local(tokens, routing, expert_in, expert_out, gain_mix, gain_out):
    ids = routing.T.reshape(1, ROWS)
    chan_pos = lax.axis_index("chan").reshape(1)
    owner = lax.axis_index(SEQ_CHAN).reshape(1)
    cols, rows = split_tokens(chan_pos, tokens)
    tables = [jnp.asarray(t) for t in (*twiddle_tables(), position_table())]
    twr, twi, tab, gain_mix, gain_out = bring(
        *tables, gain_mix.reshape(1, D), gain_out.reshape(1, D)
    )
    tc, ts = hidden_tables()
    sums = sequence_sums(owner, exchange(cols, SEQ_CHAN), twr, twi, tab)
    parts = exchange(sums, SEQ_CHAN)
    residual = []
    for i in range(1, N_CHAN):
        ring = [(c, (c + i) % N_CHAN) for c in range(N_CHAN)]
        residual.append(lax.ppermute(rows[i - 1], "chan", ring))
    normed, *outgoing = mix_rows(chan_pos, parts, tokens, residual, ids, tc, ts, gain_mix)
    back = []
    for (_, count), x in zip(CHUNKS, outgoing):
        x = exchange(x.reshape(N_SEQ, count, D), SEQ).reshape(N_SEQ * count, D)
        x = expert_rows(x, expert_in, expert_out)
        back.append(exchange(x.reshape(N_SEQ, count, D), SEQ).reshape(N_SEQ * count, D))
    return finish_rows(back, normed, ids, gain_out).reshape(DOCS, QUARTER, D)


def solution(mesh):
    torus = Mesh(
        mesh.devices.reshape(4, 4, 2, mesh.shape["chan"]), ("seq_0", "seq_1", "seq_2", "chan")
    )
    return jax.shard_map(
        local,
        mesh=torus,
        in_specs=(
            P(None, SEQ, "chan"),
            P(SEQ_CHAN, None),
            P(SEQ, None, None),
            P(SEQ, None, None),
            P(),
            P(),
        ),
        out_specs=P(None, SEQ_CHAN, None),
        check_vma=False,
    )
```

```python
import math

import jax
import jax.numpy as jnp
import numpy as np
from jax import lax
from jax.experimental import pallas as pl
from jax.experimental.pallas import tpu as pltpu
from jax.sharding import Mesh
from jax.sharding import PartitionSpec as P

SEQ = ("seq_0", "seq_1", "seq_2")
SEQ_CHAN = ("seq_0", "seq_1", "seq_2", "chan")

D = 1024
L = 8192
DOCS = 4
N_SEQ = 32
N_CHAN = 4
N_ALL = N_SEQ * N_CHAN
POS = L // N_SEQ
CH = D // N_CHAN
QUARTER = POS // N_CHAN
ROWS = DOCS * QUARTER
CH_OWN = CH // N_ALL
LANES = N_SEQ * DOCS * CH_OWN
PARTS = 8
SLOTS = 24
F32 = jnp.float32
BF16 = jnp.bfloat16
NN = (((1,), (0,)), ((), ()))
NT = (((1,), (1,)), ((), ()))
TN = (((0,), (0,)), ((), ()))


def mm(a, b, dims):
    return lax.dot_general(a, b, dims, preferred_element_type=F32)


def in_hbm(x):
    return pltpu.with_memory_space_constraint(x, pltpu.HBM)


def kernel_params(mib):
    return pltpu.CompilerParams(vmem_limit_bytes=mib << 20)


def twiddle_tables():
    k = np.arange(N_SEQ)[:, None]
    j = np.arange(POS)[None, :]
    angle = 2.0 * np.pi * ((k * j) % L) / L
    scale = 1.0 / math.sqrt(L)
    return (
        (np.cos(angle) * scale).astype(np.float32),
        (-np.sin(angle) * scale).astype(np.float32),
    )


def position_table():
    j = np.arange(POS)
    m = (np.arange(2)[:, None] + 2 * np.arange(POS // 2)[None, :]).reshape(-1)
    angle = 2.0 * np.pi * ((m[:, None] * j[None, :]) % POS) / POS
    cos, sin = np.cos(angle), np.sin(angle)
    return np.concatenate(
        [np.concatenate([cos, sin], 1), np.concatenate([sin, -cos], 1)], 0
    ).astype(BF16)


def slot_map(ids):
    one = (lax.broadcasted_iota(jnp.int32, (N_SEQ, ROWS), 0) == ids).astype(F32)
    earlier = (
        lax.broadcasted_iota(jnp.int32, (ROWS, ROWS), 0)
        < lax.broadcasted_iota(jnp.int32, (ROWS, ROWS), 1)
    ).astype(BF16)
    before = mm(one.astype(BF16), earlier, NN)
    rank = jnp.sum(before * one, axis=0, keepdims=True).astype(jnp.int32)
    slots = lax.broadcasted_iota(jnp.int32, (N_SEQ * SLOTS, ROWS), 0)
    return (slots == ids * SLOTS + rank).astype(BF16)


def tables_kernel(ids_ref, tc_ref, ts_ref, map_ref):
    map_ref[...] = slot_map(ids_ref[...])
    block = 128
    f = lax.broadcasted_iota(jnp.int32, (block, D // 2), 1)
    for i in range(D // 2 // block):
        owner = lax.broadcasted_iota(jnp.int32, (block, D // 2), 0)
        d = i // CH_OWN * CH + CH_OWN * owner + i % CH_OWN
        turn = (d * f) % D
        turn = jnp.where(turn >= D // 2, turn - D, turn)
        angle = turn.astype(F32) * (2.0 * math.pi / D)
        factor = 1.0 / math.sqrt(D)
        rows = slice(i * block, (i + 1) * block)
        tc_ref[rows, :] = (jnp.cos(angle) * factor).astype(BF16)
        ts_ref[rows, :] = (-jnp.sin(angle) * factor).astype(BF16)


def make_tables(ids):
    return pl.pallas_call(
        tables_kernel,
        out_shape=(
            jax.ShapeDtypeStruct((D // 2, D // 2), BF16),
            jax.ShapeDtypeStruct((D // 2, D // 2), BF16),
            jax.ShapeDtypeStruct((N_SEQ * SLOTS, ROWS), BF16),
        ),
        compiler_params=kernel_params(8),
        name="make_tables",
    )(ids)


def split_kernel(tok_hbm, col_ref, *refs):
    *row_refs, tok_ref, s_ref, sem = refs
    chan = lax.axis_index("chan")
    moves = [
        pltpu.make_async_copy(tok_hbm.at[doc], tok_ref.at[doc], sem.at[doc]) for doc in range(DOCS)
    ]
    for move in moves:
        move.start()
    row = lax.broadcasted_iota(jnp.int32, (CH, CH), 0)
    index = CH_OWN * (row % N_ALL) + row // N_ALL
    index = jnp.where(chan < N_CHAN // 2, index, (CH - index) % CH)
    pick = (lax.broadcasted_iota(jnp.int32, (CH, CH), 1) == index).astype(BF16)
    for doc in range(DOCS):
        moves[doc].wait()
        flipped = mm(pick, tok_ref[doc], NT)
        for j in range(CH_OWN):
            for h in range(POS // 128):
                s_ref[h, pl.ds(doc * CH_OWN + j, N_ALL, stride=PARTS), :] = flipped[
                    j * N_ALL : (j + 1) * N_ALL, h * 128 : (h + 1) * 128
                ]
    for h in range(POS // 128):
        col_ref[:, :, h * 128 : (h + 1) * 128] = (
            s_ref[h].reshape(N_ALL, PARTS, 128).astype(BF16)
        )
    for i, row_ref in enumerate(row_refs):
        first = pl.multiple_of((chan + i + 1) % N_CHAN * QUARTER, QUARTER)
        for doc in range(DOCS):
            row_ref[doc * QUARTER : (doc + 1) * QUARTER, :] = tok_ref[
                doc, pl.ds(first, QUARTER), :
            ]


def split_tokens(tokens):
    cols, *rows = pl.pallas_call(
        split_kernel,
        out_shape=(
            jax.ShapeDtypeStruct((N_ALL, PARTS, POS), BF16),
            *(jax.ShapeDtypeStruct((ROWS, CH), BF16) for _ in range(N_CHAN - 1)),
        ),
        in_specs=[pl.BlockSpec(memory_space=pltpu.HBM)],
        scratch_shapes=[
            pltpu.VMEM((DOCS, POS, CH), BF16),
            pltpu.VMEM((POS // 128, N_ALL * PARTS, 128), F32),
            pltpu.SemaphoreType.DMA((DOCS,)),
        ],
        compiler_params=kernel_params(8),
        name="split_tokens",
    )(in_hbm(tokens))
    return cols, rows


def bring_kernel(*refs):
    n = (len(refs) - 1) // 2
    moves = [pltpu.make_async_copy(refs[i], refs[n + i], refs[-1].at[i]) for i in range(n)]
    for move in moves:
        move.start()
    for move in moves:
        move.wait()


def bring(*arrays):
    return pl.pallas_call(
        bring_kernel,
        out_shape=tuple(jax.ShapeDtypeStruct(t.shape, t.dtype) for t in arrays),
        in_specs=[pl.BlockSpec(memory_space=pltpu.HBM)] * len(arrays),
        scratch_shapes=[pltpu.SemaphoreType.DMA((len(arrays),))],
        compiler_params=kernel_params(4),
        name="bring",
    )(*map(in_hbm, arrays))


def real_fft(x):
    n = len(x)
    if n == 1:
        return [(x[0], None)]
    even = real_fft(x[0::2])
    odd = real_fft(x[1::2])
    if n == 2:
        return [(even[0][0] + odd[0][0], None), (even[0][0] - odd[0][0], None)]
    out = [None] * (n // 2 + 1)
    for k in range(n // 4 + 1):
        er, ei = even[k]
        orr, oi = odd[k]
        if k == 0:
            out[0] = (er + orr, None)
            out[n // 2] = (er - orr, None)
        elif 4 * k == n:
            out[k] = (er, -orr)
        else:
            c = math.cos(2.0 * math.pi * k / n)
            s = -math.sin(2.0 * math.pi * k / n)
            if 8 * k == n:
                tr, ti = (orr + oi) * c, (oi - orr) * c
            else:
                tr, ti = orr * c - oi * s, orr * s + oi * c
            out[k] = (er + tr, ei + ti)
            out[n // 2 - k] = (er - tr, ti - ei)
    return out


def sequence_kernel(x_ref, twr_ref, twi_ref, tab_ref, out_ref, t_ref, s_ref):
    rows = DOCS * CH_OWN
    own_mirror = (lax.broadcasted_iota(jnp.int32, (rows, 128), 0) % CH_OWN == 0) & (
        lax.axis_index(SEQ_CHAN) == 0
    )

    def folded(g, s, lanes):
        third = x_ref[N_CHAN * s + 2, :, lanes].astype(F32)
        fourth = x_ref[N_CHAN * s + 3, :, lanes].astype(F32)
        base = x_ref[N_CHAN * s + g // 2, :, lanes].astype(F32)
        if g == 0:
            return base + jnp.where(own_mirror, 0.0, fourth)
        if g == 1:
            return jnp.where(own_mirror, third, base - fourth)
        other = jnp.where(own_mirror, fourth, third)
        return base + other if g == 2 else base - other

    for g in range(4):
        for half in range(POS // 128):
            lanes = slice(half * 128, (half + 1) * 128)
            lanes_im = slice(POS + half * 128, POS + (half + 1) * 128)
            freq = real_fft([folded(g, s, lanes) for s in range(N_SEQ)])
            for k in range(N_SEQ):
                if k <= N_SEQ // 2:
                    fr, fi = freq[k]
                else:
                    fr, fi = freq[N_SEQ - k]
                    fi = -fi
                wr = twr_ref[k : k + 1, lanes]
                wi = twi_ref[k : k + 1, lanes]
                if fi is None:
                    tr, ti = fr * wr, fr * wi
                else:
                    tr, ti = fr * wr - fi * wi, fr * wi + fi * wr
                if g == 1:
                    tr, ti = jnp.where(own_mirror, ti, tr), jnp.where(own_mirror, -tr, ti)
                t_ref[g, k * rows : (k + 1) * rows, lanes] = tr
                t_ref[g, k * rows : (k + 1) * rows, lanes_im] = ti
    for g in range(4):
        kind = slice(g % 2 * POS, (g % 2 + 1) * POS)
        part = mm(tab_ref[kind, :], t_ref[g].astype(BF16), NT)
        for parity in range(2):
            for h in range(LANES // 128):
                s_ref[h, pl.ds(2 * g + parity, N_ALL, stride=PARTS), :] = part[
                    parity * N_ALL : (parity + 1) * N_ALL, h * 128 : (h + 1) * 128
                ]
    for h in range(LANES // 128):
        out_ref[:, :, h * 128 : (h + 1) * 128] = (
            s_ref[h].reshape(N_ALL, PARTS, 128).astype(BF16)
        )


def sequence_sums(cols, twr, twi, tab):
    return pl.pallas_call(
        sequence_kernel,
        out_shape=jax.ShapeDtypeStruct((N_ALL, PARTS, LANES), BF16),
        scratch_shapes=[
            pltpu.VMEM((4, LANES, 2 * POS), F32),
            pltpu.VMEM((LANES // 128, N_ALL * PARTS, 128), F32),
        ],
        compiler_params=kernel_params(24),
        name="sequence_sums",
    )(cols, twr, twi, tab)


def norm_rows(values, gain):
    center = values - jnp.mean(values, axis=-1, keepdims=True)
    spread = jnp.mean(center * center, axis=-1, keepdims=True)
    return center * lax.rsqrt(spread + 1e-05) * gain


def mix_kernel(r_ref, tok_hbm, *refs):
    res_refs, rest = refs[: N_CHAN - 1], refs[N_CHAN - 1 :]
    slot_ref, tc_ref, ts_ref, gain_ref, normed_ref, out_ref, s_ref, a_ref, x_ref, sem = rest
    chan = lax.axis_index("chan")
    first = pl.multiple_of(chan * QUARTER, QUARTER)
    moves = [
        pltpu.make_async_copy(
            tok_hbm.at[doc, pl.ds(first, QUARTER), :],
            x_ref.at[chan, pl.ds(doc * QUARTER, QUARTER), :],
            sem.at[N_CHAN - 1 + doc],
        )
        for doc in range(DOCS)
    ] + [
        pltpu.make_async_copy(res_ref, x_ref.at[(chan + N_CHAN - 1 - i) % N_CHAN], sem.at[i])
        for i, res_ref in enumerate(res_refs)
    ]
    for move in moves:
        move.start()
    for h in range(LANES // 128):
        s_ref[h] = r_ref[:, :, h * 128 : (h + 1) * 128].astype(F32).reshape(N_ALL * PARTS, 128)
    row = lax.broadcasted_iota(jnp.int32, (LANES, LANES), 0)
    at = row % N_SEQ * (DOCS * CH_OWN) + row // N_SEQ % DOCS * CH_OWN + row // (N_SEQ * DOCS)
    perm = (lax.broadcasted_iota(jnp.int32, (LANES, LANES), 1) == at).astype(BF16)
    half = D // 2
    for r in range(PARTS):
        g, parity = r // 2, r % 2
        block = jnp.concatenate(
            [s_ref[h, pl.ds(r, N_ALL, stride=PARTS), :] for h in range(LANES // 128)], axis=1
        ).astype(BF16)
        flipped = mm(perm, block, NT).astype(BF16)
        for j in range(CH_OWN):
            base = g % 2 * half + g // 2 * CH + j * N_ALL
            for doc in range(DOCS):
                first = (doc * 2 + parity) * N_SEQ
                start = (j * DOCS + doc) * N_SEQ
                a_ref[first : first + N_SEQ, base : base + N_ALL] = flipped[start : start + N_SEQ]
    factor = 1.0 / math.sqrt(D)
    own = a_ref[:, half : half + 1].astype(F32) * factor
    swing = 1.0 - 2.0 * (lax.broadcasted_iota(jnp.int32, (ROWS, half), 1) % 2).astype(F32)
    cos_part = mm(a_ref[:, :half], tc_ref[...], NN) + own * swing
    sin_part = mm(a_ref[:, half:], ts_ref[...], NN)
    sign = jnp.where(
        lax.broadcasted_iota(jnp.int32, (half, 128), 0) // N_ALL % CH_OWN == 0, factor, -factor
    )
    middle = mm(a_ref[:, :half], sign.astype(BF16), NN)[:, :1] + own
    mirror = (
        lax.broadcasted_iota(jnp.int32, (half, half), 0)
        + lax.broadcasted_iota(jnp.int32, (half, half), 1)
        == half
    ).astype(BF16)
    low = (cos_part + sin_part).astype(BF16).astype(F32)
    high = mm((cos_part - sin_part).astype(BF16), mirror, NN)
    first = lax.broadcasted_iota(jnp.int32, (ROWS, half), 1) == 0
    high = jnp.where(first, middle.astype(BF16).astype(F32), high)
    mixing = jnp.concatenate([low, high], axis=1)
    for move in moves:
        move.wait()
    residual = jnp.concatenate([x_ref[c].astype(F32) for c in range(N_CHAN)], axis=1)
    normed = norm_rows(residual + mixing, gain_ref[...]).astype(BF16)
    normed_ref[...] = normed
    out_ref[...] = mm(slot_ref[...], normed, NN).astype(BF16)


def mix_rows(parts, tokens, residual, slot, tc, ts, gain):
    return pl.pallas_call(
        mix_kernel,
        out_shape=(
            jax.ShapeDtypeStruct((ROWS, D), BF16),
            jax.ShapeDtypeStruct((N_SEQ * SLOTS, D), BF16),
        ),
        scratch_shapes=[
            pltpu.VMEM((LANES // 128, N_ALL * PARTS, 128), F32),
            pltpu.VMEM((ROWS, D), BF16),
            pltpu.VMEM((N_CHAN, ROWS, CH), BF16),
            pltpu.SemaphoreType.DMA((N_CHAN - 1 + DOCS,)),
        ],
        in_specs=[pl.BlockSpec(memory_space=pltpu.VMEM)]
        + [pl.BlockSpec(memory_space=pltpu.HBM)] * N_CHAN
        + [pl.BlockSpec(memory_space=pltpu.VMEM)] * 4,
        compiler_params=kernel_params(24),
        name="mix_rows",
    )(parts, *map(in_hbm, (tokens, *residual)), slot, tc, ts, gain)


def gelu(v):
    inner = math.sqrt(2.0 / math.pi)
    return (0.5 * v) * (1.0 + jnp.tanh(v * (inner + (inner * 0.044715) * (v * v))))


def expert_kernel(x_ref, wi_hbm, wo_hbm, out_ref, wi_ref, wo_ref, h_ref, sem):
    ff = wi_ref.shape[1]
    pieces, block, width = 8, 1024, 256
    step = ff // pieces
    moves = [
        pltpu.make_async_copy(
            wi_hbm.at[0, :, i * step : (i + 1) * step], wi_ref.at[:, i * step : (i + 1) * step], sem.at[i]
        )
        for i in range(pieces)
    ] + [
        pltpu.make_async_copy(
            wo_hbm.at[0, i * step : (i + 1) * step], wo_ref.at[i * step : (i + 1) * step], sem.at[pieces + i]
        )
        for i in range(pieces)
    ]
    for move in moves:
        move.start()
    for i in range(ff // block):
        for j in range(i * block // step, (i + 1) * block // step):
            moves[j].wait()
        cols = slice(i * block, (i + 1) * block)
        h_ref[:, cols] = gelu(mm(x_ref[...], wi_ref[:, cols], NN)).astype(BF16)
    for move in moves[pieces:]:
        move.wait()
    for n in range(D // width):
        cols = slice(n * width, (n + 1) * width)
        out_ref[:, cols] = mm(h_ref[...], wo_ref[:, cols], NN).astype(BF16)


def expert_rows(x, expert_in, expert_out):
    rows, ff = x.shape[0], expert_in.shape[2]
    return pl.pallas_call(
        expert_kernel,
        out_shape=jax.ShapeDtypeStruct((rows, D), BF16),
        in_specs=[pl.BlockSpec(memory_space=pltpu.VMEM)]
        + [pl.BlockSpec(memory_space=pltpu.HBM)] * 2,
        scratch_shapes=[
            pltpu.VMEM((D, ff), BF16),
            pltpu.VMEM((ff, D), BF16),
            pltpu.VMEM((rows, ff), BF16),
            pltpu.SemaphoreType.DMA((16,)),
        ],
        compiler_params=kernel_params(40),
        name="expert_rows",
    )(x, in_hbm(expert_in), in_hbm(expert_out))


def finish_kernel(back_ref, normed_ref, slot_ref, gain_ref, out_hbm, out_ref, sem):
    half = ROWS // 2
    moves = []
    for i in range(2):
        rows = slice(i * half, (i + 1) * half)
        values = normed_ref[rows, :].astype(F32) + mm(slot_ref[:, rows], back_ref[...], TN)
        out_ref[rows, :] = norm_rows(values, gain_ref[...]).astype(BF16)
        moves.append(pltpu.make_async_copy(out_ref.at[rows], out_hbm.at[rows], sem.at[i]))
        moves[i].start()
    for move in moves:
        move.wait()


def finish_rows(back, normed, slot, gain):
    return pl.pallas_call(
        finish_kernel,
        out_shape=jax.ShapeDtypeStruct((ROWS, D), BF16),
        out_specs=pl.BlockSpec(memory_space=pltpu.HBM),
        scratch_shapes=[pltpu.VMEM((ROWS, D), BF16), pltpu.SemaphoreType.DMA((2,))],
        compiler_params=kernel_params(24),
        name="finish_rows",
    )(back, normed, slot, gain)


def exchange(x, axes):
    return lax.all_to_all(x, axes, split_axis=0, concat_axis=0, tiled=True)


def local(tokens, routing, expert_in, expert_out, gain_mix, gain_out):
    ids = routing.T.reshape(1, ROWS)
    cols, rows = split_tokens(tokens)
    tables = [jnp.asarray(t) for t in (*twiddle_tables(), position_table())]
    twr, twi, tab, gain_mix, gain_out = bring(
        *tables, gain_mix.reshape(1, D), gain_out.reshape(1, D)
    )
    tc, ts, slot = make_tables(ids)
    sums = sequence_sums(exchange(cols, SEQ_CHAN), twr, twi, tab)
    parts = exchange(sums, SEQ_CHAN)
    residual = []
    for i in range(1, N_CHAN):
        ring = [(c, (c + i) % N_CHAN) for c in range(N_CHAN)]
        residual.append(lax.ppermute(rows[i - 1], "chan", ring))
    normed, outgoing = mix_rows(parts, tokens, residual, slot, tc, ts, gain_mix)
    there = exchange(outgoing.reshape(N_SEQ, SLOTS, D), SEQ)
    result = expert_rows(there.reshape(N_SEQ * SLOTS, D), expert_in, expert_out)
    back = exchange(result.reshape(N_SEQ, SLOTS, D), SEQ)
    out = finish_rows(back.reshape(N_SEQ * SLOTS, D), normed, slot, gain_out)
    return out.reshape(DOCS, QUARTER, D)


def solution(mesh):
    torus = Mesh(
        mesh.devices.reshape(4, 4, 2, mesh.shape["chan"]), ("seq_0", "seq_1", "seq_2", "chan")
    )
    return jax.shard_map(
        local,
        mesh=torus,
        in_specs=(
            P(None, SEQ, "chan"),
            P(SEQ_CHAN, None),
            P(SEQ, None, None),
            P(SEQ, None, None),
            P(),
            P(),
        ),
        out_specs=P(None, SEQ_CHAN, None),
        check_vma=False,
    )
```

```python
import math

import jax
import jax.numpy as jnp
import numpy as np
from jax import lax
from jax.experimental import pallas as pl
from jax.experimental.pallas import tpu as pltpu
from jax.sharding import Mesh
from jax.sharding import PartitionSpec as P

SEQ = ("seq_0", "seq_1", "seq_2")
SEQ_CHAN = ("seq_0", "seq_1", "seq_2", "chan")

D = 1024
L = 8192
DOCS = 4
N_SEQ = 32
N_CHAN = 4
N_ALL = N_SEQ * N_CHAN
POS = L // N_SEQ
CH = D // N_CHAN
QUARTER = POS // N_CHAN
ROWS = DOCS * QUARTER
CH_OWN = CH // N_ALL
LANES = N_SEQ * DOCS * CH_OWN
PARTS = 8
SLOTS = 24
F32 = jnp.float32
BF16 = jnp.bfloat16
NN = (((1,), (0,)), ((), ()))
NT = (((1,), (1,)), ((), ()))
TN = (((0,), (0,)), ((), ()))


def mm(a, b, dims):
    return lax.dot_general(a, b, dims, preferred_element_type=F32)


def in_hbm(x):
    return pltpu.with_memory_space_constraint(x, pltpu.HBM)


def kernel_params(mib):
    return pltpu.CompilerParams(vmem_limit_bytes=mib << 20)


def twiddle_tables():
    k = np.arange(N_SEQ)[:, None]
    j = np.arange(POS)[None, :]
    angle = 2.0 * np.pi * ((k * j) % L) / L
    scale = 1.0 / math.sqrt(L)
    return (
        (np.cos(angle) * scale).astype(np.float32),
        (-np.sin(angle) * scale).astype(np.float32),
    )


def position_table():
    j = np.arange(POS)
    m = (np.arange(2)[:, None] + 2 * np.arange(POS // 2)[None, :]).reshape(-1)
    angle = 2.0 * np.pi * ((m[:, None] * j[None, :]) % POS) / POS
    cos, sin = np.cos(angle), np.sin(angle)
    return np.concatenate(
        [np.concatenate([cos, sin], 1), np.concatenate([sin, -cos], 1)], 0
    ).astype(BF16)


def slot_map(ids):
    one = (lax.broadcasted_iota(jnp.int32, (N_SEQ, ROWS), 0) == ids).astype(F32)
    earlier = (
        lax.broadcasted_iota(jnp.int32, (ROWS, ROWS), 0)
        < lax.broadcasted_iota(jnp.int32, (ROWS, ROWS), 1)
    ).astype(BF16)
    before = mm(one.astype(BF16), earlier, NN)
    rank = jnp.sum(before * one, axis=0, keepdims=True).astype(jnp.int32)
    slots = lax.broadcasted_iota(jnp.int32, (N_SEQ * SLOTS, ROWS), 0)
    return (slots == ids * SLOTS + rank).astype(BF16)


def tables_kernel(ids_ref, tc_ref, ts_ref, map_ref):
    map_ref[...] = slot_map(ids_ref[...])
    block = 128
    f = lax.broadcasted_iota(jnp.int32, (block, D // 2), 1)
    for i in range(D // 2 // block):
        owner = lax.broadcasted_iota(jnp.int32, (block, D // 2), 0)
        d = i // CH_OWN * CH + CH_OWN * owner + i % CH_OWN
        turn = (d * f) % D
        turn = jnp.where(turn >= D // 2, turn - D, turn)
        angle = turn.astype(F32) * (2.0 * math.pi / D)
        factor = 1.0 / math.sqrt(D)
        rows = slice(i * block, (i + 1) * block)
        tc_ref[rows, :] = (jnp.cos(angle) * factor).astype(BF16)
        ts_ref[rows, :] = (-jnp.sin(angle) * factor).astype(BF16)


def make_tables(ids):
    return pl.pallas_call(
        tables_kernel,
        out_shape=(
            jax.ShapeDtypeStruct((D // 2, D // 2), BF16),
            jax.ShapeDtypeStruct((D // 2, D // 2), BF16),
            jax.ShapeDtypeStruct((N_SEQ * SLOTS, ROWS), BF16),
        ),
        compiler_params=kernel_params(8),
        name="make_tables",
    )(ids)


def split_kernel(tok_ref, col_ref, s_ref):
    chan = lax.axis_index("chan")
    row = lax.broadcasted_iota(jnp.int32, (CH, CH), 0)
    index = CH_OWN * (row % N_ALL) + row // N_ALL
    index = jnp.where(chan < N_CHAN // 2, index, (CH - index) % CH)
    pick = (lax.broadcasted_iota(jnp.int32, (CH, CH), 1) == index).astype(BF16)
    for doc in range(DOCS):
        flipped = mm(pick, tok_ref[doc], NT)
        for j in range(CH_OWN):
            for h in range(POS // 128):
                s_ref[h, pl.ds(doc * CH_OWN + j, N_ALL, stride=PARTS), :] = flipped[
                    j * N_ALL : (j + 1) * N_ALL, h * 128 : (h + 1) * 128
                ]
    for h in range(POS // 128):
        col_ref[:, :, h * 128 : (h + 1) * 128] = (
            s_ref[h].reshape(N_ALL, PARTS, 128).astype(BF16)
        )


def split_tokens(tokens):
    return pl.pallas_call(
        split_kernel,
        out_shape=jax.ShapeDtypeStruct((N_ALL, PARTS, POS), BF16),
        scratch_shapes=[
            pltpu.VMEM((POS // 128, N_ALL * PARTS, 128), F32),
        ],
        compiler_params=kernel_params(8),
        name="split_tokens",
    )(tokens)


def cut_kernel(tok_hbm, *refs):
    *row_hbms, sem = refs
    moves = []
    for i, row_hbm in enumerate(row_hbms):
        first = pl.multiple_of((lax.axis_index("chan") + i + 1) % N_CHAN * QUARTER, QUARTER)
        for doc in range(DOCS):
            moves.append(
                pltpu.make_async_copy(
                    tok_hbm.at[doc, pl.ds(first, QUARTER), :],
                    row_hbm.at[pl.ds(doc * QUARTER, QUARTER), :],
                    sem.at[len(moves)],
                )
            )
    for move in moves:
        move.start()
    for move in moves:
        move.wait()


def cut_rows(tokens):
    return pl.pallas_call(
        cut_kernel,
        out_shape=tuple(jax.ShapeDtypeStruct((ROWS, CH), BF16) for _ in range(N_CHAN - 1)),
        in_specs=[pl.BlockSpec(memory_space=pltpu.HBM)],
        out_specs=(pl.BlockSpec(memory_space=pltpu.HBM),) * (N_CHAN - 1),
        scratch_shapes=[pltpu.SemaphoreType.DMA(((N_CHAN - 1) * DOCS,))],
        compiler_params=kernel_params(4),
        name="cut_rows",
    )(in_hbm(tokens))


def bring_kernel(*refs):
    n = (len(refs) - 1) // 2
    moves = [pltpu.make_async_copy(refs[i], refs[n + i], refs[-1].at[i]) for i in range(n)]
    for move in moves:
        move.start()
    for move in moves:
        move.wait()


def bring(*arrays):
    return pl.pallas_call(
        bring_kernel,
        out_shape=tuple(jax.ShapeDtypeStruct(t.shape, t.dtype) for t in arrays),
        in_specs=[pl.BlockSpec(memory_space=pltpu.HBM)] * len(arrays),
        scratch_shapes=[pltpu.SemaphoreType.DMA((len(arrays),))],
        compiler_params=kernel_params(4),
        name="bring",
    )(*map(in_hbm, arrays))


def real_fft(x):
    n = len(x)
    if n == 1:
        return [(x[0], None)]
    even = real_fft(x[0::2])
    odd = real_fft(x[1::2])
    if n == 2:
        return [(even[0][0] + odd[0][0], None), (even[0][0] - odd[0][0], None)]
    out = [None] * (n // 2 + 1)
    for k in range(n // 4 + 1):
        er, ei = even[k]
        orr, oi = odd[k]
        if k == 0:
            out[0] = (er + orr, None)
            out[n // 2] = (er - orr, None)
        elif 4 * k == n:
            out[k] = (er, -orr)
        else:
            c = math.cos(2.0 * math.pi * k / n)
            s = -math.sin(2.0 * math.pi * k / n)
            if 8 * k == n:
                tr, ti = (orr + oi) * c, (oi - orr) * c
            else:
                tr, ti = orr * c - oi * s, orr * s + oi * c
            out[k] = (er + tr, ei + ti)
            out[n // 2 - k] = (er - tr, ti - ei)
    return out


def sequence_kernel(x_ref, twr_ref, twi_ref, tab_ref, out_ref, t_ref, s_ref):
    rows = DOCS * CH_OWN
    own_mirror = (lax.broadcasted_iota(jnp.int32, (rows, 128), 0) % CH_OWN == 0) & (
        lax.axis_index(SEQ_CHAN) == 0
    )

    def folded(g, s, lanes):
        third = x_ref[N_CHAN * s + 2, :, lanes].astype(F32)
        fourth = x_ref[N_CHAN * s + 3, :, lanes].astype(F32)
        base = x_ref[N_CHAN * s + g // 2, :, lanes].astype(F32)
        if g == 0:
            return base + jnp.where(own_mirror, 0.0, fourth)
        if g == 1:
            return jnp.where(own_mirror, third, base - fourth)
        other = jnp.where(own_mirror, fourth, third)
        return base + other if g == 2 else base - other

    for g in range(4):
        for half in range(POS // 128):
            lanes = slice(half * 128, (half + 1) * 128)
            lanes_im = slice(POS + half * 128, POS + (half + 1) * 128)
            freq = real_fft([folded(g, s, lanes) for s in range(N_SEQ)])
            for k in range(N_SEQ):
                if k <= N_SEQ // 2:
                    fr, fi = freq[k]
                else:
                    fr, fi = freq[N_SEQ - k]
                    fi = -fi
                wr = twr_ref[k : k + 1, lanes]
                wi = twi_ref[k : k + 1, lanes]
                if fi is None:
                    tr, ti = fr * wr, fr * wi
                else:
                    tr, ti = fr * wr - fi * wi, fr * wi + fi * wr
                if g == 1:
                    tr, ti = jnp.where(own_mirror, ti, tr), jnp.where(own_mirror, -tr, ti)
                t_ref[g, k * rows : (k + 1) * rows, lanes] = tr
                t_ref[g, k * rows : (k + 1) * rows, lanes_im] = ti
    for g in range(4):
        kind = slice(g % 2 * POS, (g % 2 + 1) * POS)
        part = mm(tab_ref[kind, :], t_ref[g].astype(BF16), NT)
        for parity in range(2):
            for h in range(LANES // 128):
                s_ref[h, pl.ds(2 * g + parity, N_ALL, stride=PARTS), :] = part[
                    parity * N_ALL : (parity + 1) * N_ALL, h * 128 : (h + 1) * 128
                ]
    for h in range(LANES // 128):
        out_ref[:, :, h * 128 : (h + 1) * 128] = (
            s_ref[h].reshape(N_ALL, PARTS, 128).astype(BF16)
        )


def sequence_sums(cols, twr, twi, tab):
    return pl.pallas_call(
        sequence_kernel,
        out_shape=jax.ShapeDtypeStruct((N_ALL, PARTS, LANES), BF16),
        scratch_shapes=[
            pltpu.VMEM((4, LANES, 2 * POS), F32),
            pltpu.VMEM((LANES // 128, N_ALL * PARTS, 128), F32),
        ],
        compiler_params=kernel_params(24),
        name="sequence_sums",
    )(cols, twr, twi, tab)


def norm_rows(values, gain):
    center = values - jnp.mean(values, axis=-1, keepdims=True)
    spread = jnp.mean(center * center, axis=-1, keepdims=True)
    return center * lax.rsqrt(spread + 1e-05) * gain


def mix_kernel(r_ref, tok_hbm, *refs):
    res_refs, rest = refs[: N_CHAN - 1], refs[N_CHAN - 1 :]
    slot_ref, tc_ref, ts_ref, gain_ref, normed_ref, out_ref, s_ref, a_ref, x_ref, sem = rest
    chan = lax.axis_index("chan")
    first = pl.multiple_of(chan * QUARTER, QUARTER)
    moves = [
        pltpu.make_async_copy(
            tok_hbm.at[doc, pl.ds(first, QUARTER), :],
            x_ref.at[chan, pl.ds(doc * QUARTER, QUARTER), :],
            sem.at[N_CHAN - 1 + doc],
        )
        for doc in range(DOCS)
    ] + [
        pltpu.make_async_copy(res_ref, x_ref.at[(chan + N_CHAN - 1 - i) % N_CHAN], sem.at[i])
        for i, res_ref in enumerate(res_refs)
    ]
    for move in moves:
        move.start()
    for h in range(LANES // 128):
        s_ref[h] = r_ref[:, :, h * 128 : (h + 1) * 128].astype(F32).reshape(N_ALL * PARTS, 128)
    row = lax.broadcasted_iota(jnp.int32, (LANES, LANES), 0)
    at = row % N_SEQ * (DOCS * CH_OWN) + row // N_SEQ % DOCS * CH_OWN + row // (N_SEQ * DOCS)
    perm = (lax.broadcasted_iota(jnp.int32, (LANES, LANES), 1) == at).astype(BF16)
    half = D // 2
    for r in range(PARTS):
        g, parity = r // 2, r % 2
        block = jnp.concatenate(
            [s_ref[h, pl.ds(r, N_ALL, stride=PARTS), :] for h in range(LANES // 128)], axis=1
        ).astype(BF16)
        flipped = mm(perm, block, NT).astype(BF16)
        for j in range(CH_OWN):
            base = g % 2 * half + g // 2 * CH + j * N_ALL
            for doc in range(DOCS):
                first = (doc * 2 + parity) * N_SEQ
                start = (j * DOCS + doc) * N_SEQ
                a_ref[first : first + N_SEQ, base : base + N_ALL] = flipped[start : start + N_SEQ]
    factor = 1.0 / math.sqrt(D)
    own = a_ref[:, half : half + 1].astype(F32) * factor
    swing = 1.0 - 2.0 * (lax.broadcasted_iota(jnp.int32, (ROWS, half), 1) % 2).astype(F32)
    cos_part = mm(a_ref[:, :half], tc_ref[...], NN) + own * swing
    sin_part = mm(a_ref[:, half:], ts_ref[...], NN)
    sign = jnp.where(
        lax.broadcasted_iota(jnp.int32, (half, 128), 0) // N_ALL % CH_OWN == 0, factor, -factor
    )
    middle = mm(a_ref[:, :half], sign.astype(BF16), NN)[:, :1] + own
    mirror = (
        lax.broadcasted_iota(jnp.int32, (half, half), 0)
        + lax.broadcasted_iota(jnp.int32, (half, half), 1)
        == half
    ).astype(BF16)
    low = (cos_part + sin_part).astype(BF16).astype(F32)
    high = mm((cos_part - sin_part).astype(BF16), mirror, NN)
    first = lax.broadcasted_iota(jnp.int32, (ROWS, half), 1) == 0
    high = jnp.where(first, middle.astype(BF16).astype(F32), high)
    mixing = jnp.concatenate([low, high], axis=1)
    for move in moves:
        move.wait()
    residual = jnp.concatenate([x_ref[c].astype(F32) for c in range(N_CHAN)], axis=1)
    normed = norm_rows(residual + mixing, gain_ref[...]).astype(BF16)
    normed_ref[...] = normed
    out_ref[...] = mm(slot_ref[...], normed, NN).astype(BF16)


def mix_rows(parts, tokens, residual, slot, tc, ts, gain):
    return pl.pallas_call(
        mix_kernel,
        out_shape=(
            jax.ShapeDtypeStruct((ROWS, D), BF16),
            jax.ShapeDtypeStruct((N_SEQ * SLOTS, D), BF16),
        ),
        scratch_shapes=[
            pltpu.VMEM((LANES // 128, N_ALL * PARTS, 128), F32),
            pltpu.VMEM((ROWS, D), BF16),
            pltpu.VMEM((N_CHAN, ROWS, CH), BF16),
            pltpu.SemaphoreType.DMA((N_CHAN - 1 + DOCS,)),
        ],
        in_specs=[pl.BlockSpec(memory_space=pltpu.VMEM)]
        + [pl.BlockSpec(memory_space=pltpu.HBM)] * N_CHAN
        + [pl.BlockSpec(memory_space=pltpu.VMEM)] * 4,
        compiler_params=kernel_params(24),
        name="mix_rows",
    )(parts, *map(in_hbm, (tokens, *residual)), slot, tc, ts, gain)


def gelu(v):
    inner = math.sqrt(2.0 / math.pi)
    return (0.5 * v) * (1.0 + jnp.tanh(v * (inner + (inner * 0.044715) * (v * v))))


def expert_kernel(x_ref, wi_hbm, wo_hbm, out_ref, wi_ref, wo_ref, h_ref, sem):
    ff = wi_ref.shape[1]
    pieces, width = 8, 256
    step = ff // pieces
    moves = [
        pltpu.make_async_copy(
            wi_hbm.at[0, :, i * step : (i + 1) * step], wi_ref.at[:, i * step : (i + 1) * step], sem.at[i]
        )
        for i in range(pieces)
    ] + [
        pltpu.make_async_copy(
            wo_hbm.at[0, i * step : (i + 1) * step], wo_ref.at[i * step : (i + 1) * step], sem.at[pieces + i]
        )
        for i in range(pieces)
    ]
    for move in moves:
        move.start()
    for first, count in ((0, 1), (1, 1), (2, 2), (4, 2), (6, 2)):
        for move in moves[first : first + count]:
            move.wait()
        cols = slice(first * step, (first + count) * step)
        h_ref[:, cols] = gelu(mm(x_ref[...], wi_ref[:, cols], NN)).astype(BF16)
    for move in moves[pieces:]:
        move.wait()
    for n in range(D // width):
        cols = slice(n * width, (n + 1) * width)
        out_ref[:, cols] = mm(h_ref[...], wo_ref[:, cols], NN).astype(BF16)


def expert_rows(x, expert_in, expert_out):
    rows, ff = x.shape[0], expert_in.shape[2]
    return pl.pallas_call(
        expert_kernel,
        out_shape=jax.ShapeDtypeStruct((rows, D), BF16),
        in_specs=[pl.BlockSpec(memory_space=pltpu.VMEM)]
        + [pl.BlockSpec(memory_space=pltpu.HBM)] * 2,
        scratch_shapes=[
            pltpu.VMEM((D, ff), BF16),
            pltpu.VMEM((ff, D), BF16),
            pltpu.VMEM((rows, ff), BF16),
            pltpu.SemaphoreType.DMA((16,)),
        ],
        compiler_params=kernel_params(40),
        name="expert_rows",
    )(x, in_hbm(expert_in), in_hbm(expert_out))


def finish_kernel(back_ref, normed_ref, slot_ref, gain_ref, out_hbm, out_ref, sem):
    half = ROWS // 2
    moves = []
    for i in range(2):
        rows = slice(i * half, (i + 1) * half)
        values = normed_ref[rows, :].astype(F32) + mm(slot_ref[:, rows], back_ref[...], TN)
        out_ref[rows, :] = norm_rows(values, gain_ref[...]).astype(BF16)
        moves.append(pltpu.make_async_copy(out_ref.at[rows], out_hbm.at[rows], sem.at[i]))
        moves[i].start()
    for move in moves:
        move.wait()


def finish_rows(back, normed, slot, gain):
    return pl.pallas_call(
        finish_kernel,
        out_shape=jax.ShapeDtypeStruct((ROWS, D), BF16),
        out_specs=pl.BlockSpec(memory_space=pltpu.HBM),
        scratch_shapes=[pltpu.VMEM((ROWS, D), BF16), pltpu.SemaphoreType.DMA((2,))],
        compiler_params=kernel_params(24),
        name="finish_rows",
    )(back, normed, slot, gain)


def exchange(x, axes):
    return lax.all_to_all(x, axes, split_axis=0, concat_axis=0, tiled=True)


def local(tokens, routing, expert_in, expert_out, gain_mix, gain_out):
    ids = routing.T.reshape(1, ROWS)
    cols, rows = split_tokens(tokens), cut_rows(tokens)
    tables = [jnp.asarray(t) for t in (*twiddle_tables(), position_table())]
    twr, twi, tab, gain_mix, gain_out = bring(
        *tables, gain_mix.reshape(1, D), gain_out.reshape(1, D)
    )
    tc, ts, slot = make_tables(ids)
    sums = sequence_sums(exchange(cols, SEQ_CHAN), twr, twi, tab)
    parts = exchange(sums, SEQ_CHAN)
    residual = []
    for i in range(1, N_CHAN):
        ring = [(c, (c + i) % N_CHAN) for c in range(N_CHAN)]
        residual.append(lax.ppermute(rows[i - 1], "chan", ring))
    normed, outgoing = mix_rows(parts, tokens, residual, slot, tc, ts, gain_mix)
    there = exchange(outgoing.reshape(N_SEQ, SLOTS, D), SEQ)
    result = expert_rows(there.reshape(N_SEQ * SLOTS, D), expert_in, expert_out)
    back = exchange(result.reshape(N_SEQ, SLOTS, D), SEQ)
    out = finish_rows(back.reshape(N_SEQ * SLOTS, D), normed, slot, gain_out)
    return out.reshape(DOCS, QUARTER, D)


def solution(mesh):
    torus = Mesh(
        mesh.devices.reshape(4, 4, 2, mesh.shape["chan"]), ("seq_0", "seq_1", "seq_2", "chan")
    )
    return jax.shard_map(
        local,
        mesh=torus,
        in_specs=(
            P(None, SEQ, "chan"),
            P(SEQ_CHAN, None),
            P(SEQ, None, None),
            P(SEQ, None, None),
            P(),
            P(),
        ),
        out_specs=P(None, SEQ_CHAN, None),
        check_vma=False,
    )
```
